32 devices in a mesh: segment: 4 (over z), seq: 8 (over y, x, core).
Axes of the slice: x: 2, y: 2, z: 4, core: 2. Of those that a mesh axis runs over, the one named last changes fastest.
Arguments:
- sequence: bfloat16 [256, 512, 256], P('seq', 'segment'), may hold values from -6 to 6
- first_factors: bfloat16 [4, 4, 256, 256], P('segment'), may hold values from -0.375 to 0.375
- second_factors: bfloat16 [4, 4, 256, 256], P('segment'), may hold values from -0.375 to 0.375
- kernels: bfloat16 [4, 2, 256, 256], P('segment', None, 'seq'), may hold values from -6 to 6
- gate_scale: float32 [4, 512], P('segment'), may hold values from -2 to 2
- gate_bias: float32 [4, 512], P('segment'), may hold values from -1 to 1
Outputs:
- mixed: bfloat16 [256, 512, 256], P('seq', 'segment')
The draws below stay inside these ranges and needn't reach their ends.
All inputs are finite; a program needn't handle non-finite values.
Results may differ from the reference program's by a relative error of at most 0.024.
Values may be sent and summed in bfloat16 or wider, within the bound.
A program may use at most 64 MiB of HBM per device.

```python
import jax
import jax.numpy as jnp

RADIX = 256
D = 512
LAYERS = 4


def steps_of(key, shape, pieces, least, top_value):
    level, own = 1.0, jax.random.fold_in(key, 6)
    for position, blocks in pieces:
        steps = jnp.exp(jax.random.uniform(jax.random.fold_in(own, position), (blocks,), jnp.float32, least / len(pieces), top_value / len(pieces)))
        level = level * jnp.repeat(steps, shape[position] // blocks).reshape([-1 if axis == position else 1 for axis in range(len(shape))])
    return level


def gaussian(key, extent, width, most, pieces=(), dtype=jnp.bfloat16):
    values = width * jax.random.normal(key, extent, jnp.float32)
    if pieces:
        values = values * steps_of(key, extent, pieces, -0.22, 0.18)
    return jnp.clip(values, -most, most).astype(dtype)


def setup_inputs(seed: int = 0) -> dict:
    splits = jax.random.split(jax.random.key(seed), 7)
    return {
        "sequence": gaussian(splits[0], (RADIX, D, RADIX), 1.0, 6.0, ((0, 8), (1, 4))),
        "first_factors": gaussian(splits[1], (LAYERS, 4, RADIX, RADIX), RADIX ** -0.5, 0.375, ((0, 4),)),
        "second_factors": gaussian(splits[2], (LAYERS, 4, RADIX, RADIX), RADIX ** -0.5, 0.375, ((0, 4),)),
        "kernels": gaussian(splits[3], (LAYERS, 2, RADIX, RADIX), 1.0, 6.0, ((0, 4), (2, 8))),
        "gate_scale": jnp.clip(jax.random.uniform(splits[4], (LAYERS, D), jnp.float32, -2.0, 2.0) * steps_of(splits[4], (LAYERS, D), ((0, 4),), -0.4, 0.0), -2.0, 2.0),
        "gate_bias": jnp.clip(jax.random.uniform(splits[5], (LAYERS, D), jnp.float32, -1.0, 1.0) * steps_of(splits[5], (LAYERS, D), ((0, 4),), -0.4, 0.0), -1.0, 1.0),
    }


def monarch(values, first, second):
    mixed = jnp.einsum('pcq,kq->pck', values.astype(jnp.float32), first.astype(jnp.float32)).astype(jnp.bfloat16)
    return jnp.einsum('pck,jp->kcj', mixed.astype(jnp.float32), second.astype(jnp.float32))


def layer_apply(values, first, second, kernel_pair, scales, biases):
    kernel_one = kernel_pair[0].astype(jnp.float32)[:, None, :]
    kernel_two = kernel_pair[1].astype(jnp.float32)[:, None, :]
    widened = values.astype(jnp.float32)
    branch_one = (monarch(values, first[0], second[0]) * kernel_one).astype(jnp.bfloat16)
    gating = jax.nn.sigmoid(scales[None, :, None] * widened + biases[None, :, None])
    gated = (monarch(branch_one, first[1], second[1]) * gating).astype(jnp.bfloat16)
    branch_two = (monarch(gated, first[2], second[2]) * kernel_two).astype(jnp.bfloat16)
    return (widened + monarch(branch_two, first[3], second[3])).astype(jnp.bfloat16)


def reference(sequence, first_factors, second_factors, kernels, gate_scale, gate_bias):
    current = sequence
    for level in range(LAYERS):
        current = layer_apply(current, first_factors[level], second_factors[level], kernels[level], gate_scale[level], gate_bias[level])
    return current
```

```python
import functools

import jax
import jax.numpy as jnp
from jax import lax
from jax.experimental import pallas as pl
from jax.experimental.pallas import tpu as pltpu
from jax.sharding import PartitionSpec as P

F32, BF16 = jnp.float32, jnp.bfloat16
NT = (((1,), (1,)), ((), ()))
NN = (((1,), (0,)), ((), ()))


def dot(a, b, dims):
    return lax.dot_general(a, b, dims, preferred_element_type=F32)


def halved(l, z, split):
    return split and ((l == 0 and z > 0) or (l == 1 and z == 0))


def pieces(l, z, maps, split):
    if halved(l, z, split):
        return [(j, True) for j in range(maps // 2)]
    return [(i, False) for i in range(maps)]


def step_order(layers, groups):
    early, lead = min(2, layers), min(2, groups)
    order = [(l, g) for g in range(lead) for l in range(early)]
    order += [(l, g) for g in range(lead) for l in range(early, layers)]
    order += [(l, g) for g in range(lead, groups) for l in range(layers)]
    return order


T0, WIRE, HOP, STEP, KZ, KS, READY = 5.0, 2.85, 1.4, 1.8, 7.5, 15.5, 18.0


def line_arrivals(nz, maps, split):
    arrive = [dict() for _ in range(nz)]
    sends = [[] for _ in range(nz)]
    for up in (True, False):
        path = range(nz - 1) if up else range(nz - 1, 0, -1)
        for z in path:
            to = z + 1 if up else z - 1
            own = pieces(z, to, maps, split)
            lead = len(own) if not up or z == 0 else min(1 if z == 1 else 2, len(own))
            free, queue = T0, [(T0, z, q) for q in own[:lead]]
            below = range(z) if up else range(z + 1, nz)
            relays = sorted(
                (arrive[z][l, q], l, q) for l in below for q in pieces(l, to, maps, split)
            )
            queue += relays
            last = relays[-1][0] if relays else T0
            queue += [(last, z, q) for q in own[lead:]]
            for at, l, q in queue:
                free = max(free, at) + WIRE
                arrive[to][l, q] = free + HOP
                if l == z:
                    sends[z].append((0.0 if at == T0 else at, l, q, up))
    return arrive, sends


def schedule(nz, maps, groups, split):
    order = step_order(nz, groups)
    arrive, sends = line_arrivals(nz, maps, split)
    plans = []
    for z in range(nz):
        acts = []
        spread = 0
        for (l, q), at in sorted(arrive[z].items(), key=lambda v: v[1]):
            to = z + 1 if l < z else z - 1
            passes = 0 <= to < nz and q in pieces(l, to, maps, split)
            acts.append((at - (1.2 if passes else 0.0), 1, "line", l, q, l < z))
            if halved(l, z, split):
                acts.append((max(at + 5.0, 17.0 + 1.5 * spread), 2, "other", l, q, l < z))
                spread += 1
        for at, l, q, up in sends[z]:
            acts.append((at - 1.19 if at else 0.0, 0 if not at else 3, "own", l, q, up))
        acts.append((KZ, 4, "kz", 0, (0, False), True))
        acts.append((KS, 4, "ks", 0, (0, False), True))
        swaps = max([at for (l, _), at in arrive[z].items() if halved(l, z, split)], default=0.0)
        late = swaps > 19.0
        for g in range(1, groups):
            if late:
                at = 14.0 if g == 1 else swaps + 0.5 + 5.8 * (g - 2)
            else:
                at = 16.0 + 5.6 * (g - 1)
            acts.append((at, 5, "in", g, (0, False), True))
        acts.sort()
        before = [a for a in acts if a[0] <= READY]
        rest = [a for a in acts if a[0] > READY]
        now, slots = READY, {}
        for t, (l, g) in enumerate(order):
            x_at = 0.0 if not g else 16.0 + 5.6 * g + 2.5
            while True:
                need = [a for a in rest if a[2] in ("line", "other") and a[3] == l]
                if rest and rest[0][0] <= now + 0.3:
                    slots.setdefault(t, []).append(rest.pop(0))
                elif not need and x_at <= now:
                    break
                else:
                    now = min([a[0] for a in rest[:1]] + ([x_at] if not need else []))
            now += STEP
        slots.setdefault(len(order) - 1, [])
        slots[len(order) - 1] += rest
        plans.append((before, slots))
    return order, plans


def kernel(
    n, nz, group, seq_in, f_own, g_own, k_own, scale_own, bias_own, out,
    raw, x_in, x, w, kk, scales, biases, kt, gv,
    own_sem, raw_sem, in_send, in_recv, out_send, out_recv, out_own,
    w_send, z_recv, sib_recv, kz_send, kz_recv, ks_send, ks_recv, kf_send, kf_recv,
):
    s, z = lax.axis_index("seq"), lax.axis_index("segment")
    core = lax.rem(s, 2)
    sib = s + 1 - 2 * core
    channels, _, rows, radix = x.shape
    groups = channels // group
    maps = w.shape[2]
    layers = w.shape[1]
    half = n // 2
    split = n == 8 and maps % 2 == 0 and nz > 2
    parity = lax.rem(lax.div(s, 2) + lax.div(s, 4), 2)
    beside = (s + 2 - 4 * lax.rem(lax.div(s, 2), 2), s + 4 - 8 * lax.rem(lax.div(s, 4), 2))
    order, plans = schedule(nz, maps, groups, split)

    def peer(d):
        return lax.rem(s + d, n)

    def remote(src, dst, send, recv, **where):
        return pltpu.make_async_remote_copy(
            src_ref=src, dst_ref=dst, send_sem=send, recv_sem=recv,
            device_id=where, device_id_type=pl.DeviceIdType.MESH,
        )

    def in_copy(g, d):
        t = peer(d)
        here = pl.ds(g * group, group)
        return remote(
            x_in.at[t, here], x.at[here, s], in_send, in_recv.at[g], seq=t
        )

    def out_copy(g, d):
        t = peer(d)
        here = pl.ds(g * group, group)
        return remote(
            x.at[here, t], out.at[s, here], out_send, out_recv, seq=t
        )

    def z_copy(l, i, up):
        v = w.at[core, l, i]
        return remote(v, v, w_send, z_recv.at[l, i], segment=z + 1 if up else z - 1)

    def ex_copy(l, i, j):
        v = w.at[core, l, i]
        return remote(v, v, w_send, z_recv.at[l, i], seq=beside[j % 2])

    def sib_copy(l, r):
        v = w.at[core, l, r]
        return remote(v, v, w_send, sib_recv.at[l], seq=sib)

    def sib_wait(l):
        v = w.at[1 - core, l]
        remote(v, v, w_send, sib_recv.at[l], seq=sib).wait_recv()

    def kz_copy(d, l):
        to = lax.rem(z + d, nz)
        return tuple(
            remote(v, v, kz_send.at[i], kz_recv.at[i], segment=to)
            for i, v in enumerate((kk.at[s, l], scales.at[l], biases.at[l]))
        )

    def kz_all():
        others = pl.ds(0, nz - 1)
        return tuple(
            remote(v, v, kz_send.at[i], kz_recv.at[i], segment=lax.rem(z + 1, nz))
            for i, v in enumerate((kk.at[s, others], scales.at[others], biases.at[others]))
        )

    def ks_copy(d, owner):
        v = kk.at[owner]
        return remote(v, v, ks_send, ks_recv, seq=lax.rem(s + 2 * d, n))

    def ks_all():
        v = kk.at[pl.ds(0, half - 1)]
        return remote(v, v, ks_send, ks_recv, seq=sib)

    def kf_copy(owner):
        v = kk.at[owner]
        return remote(v, v, kf_send, kf_recv, seq=sib)

    def kf_all():
        v = kk.at[pl.ds(0, half)]
        return remote(v, v, kf_send, kf_recv, seq=sib)

    def in_wait(g):
        v = x.at[pl.ds(g * group, group), pl.ds(0, n - 1)]
        remote(v, v, in_send, in_recv.at[g], seq=sib).wait_recv()

    own = [
        pltpu.make_async_copy(f_own.at[0], w.at[0, z], own_sem.at[0]),
        pltpu.make_async_copy(g_own.at[0], w.at[1, z], own_sem.at[1]),
        pltpu.make_async_copy(k_own.at[0], kk.at[s, z], own_sem.at[2]),
        pltpu.make_async_copy(scale_own, scales.at[z], own_sem.at[3]),
        pltpu.make_async_copy(bias_own, biases.at[z], own_sem.at[4]),
    ]
    def raw_copy(d):
        t = peer(d)
        return pltpu.make_async_copy(seq_in.at[:, t], raw.at[t], raw_sem.at[d])

    for c in own:
        c.start()
    for d in range(1, n + 1):
        raw_copy(d % n).start()

    barrier = pltpu.get_barrier_semaphore()
    mesh_id = pl.DeviceIdType.MESH

    def greet(d, _):
        pl.semaphore_signal(barrier, inc=1, device_id={"seq": peer(d)}, device_id_type=mesh_id)
        return 0

    lax.fori_loop(1, n, greet, 0)

    def greet_z(d, _):
        to = lax.rem(z + d, nz)
        pl.semaphore_signal(barrier, inc=1, device_id={"segment": to}, device_id_type=mesh_id)
        return 0

    lax.fori_loop(1, nz, greet_z, 0)
    pl.semaphore_wait(barrier, n + nz - 2)

    for c in own:
        c.wait()

    for d in range(1, nz):
        for c in kz_copy(d, z):
            c.start()

    def send_in(g, _):
        def one(d, _):
            in_copy(g, d).start()
            return 0

        return lax.fori_loop(1, n, one, 0)

    def turned(d):
        raw_copy(d).wait()
        v = raw[peer(d)]
        return jnp.swapaxes(v, 0, 1)

    def turn(d, _):
        x_in[peer(d)] = turned(d)

        @pl.when(d > 1)
        def _():
            in_copy(0, d - 1).start()

        return 0

    def mine(q):
        return 2 * q[0] + parity if q[1] else q[0]

    def onward(zz, l, q, up):
        to = zz + 1 if up else zz - 1
        return 0 <= to < nz and q in pieces(l, to, maps, split)

    def act(zz, kind, l, q, up):
        if kind == "own":
            z_copy(l, mine(q), up).start()
        elif kind == "line":
            i = mine(q)
            c = z_copy(l, i, up)
            c.wait_recv()
            if onward(zz, l, q, up):
                c.start()
            if halved(l, zz, split):
                ex_copy(l, i, q[0]).start()
            sib_copy(l, i).start()
        elif kind == "other":
            i = 2 * q[0] + 1 - parity
            ex_copy(l, i, q[0]).wait_recv()
            sib_copy(l, i).start()
        elif kind == "kz":
            for c in kz_all():
                c.wait_recv()
            for d in range(1, half):
                ks_copy(d, s).start()
            kf_copy(s).start()
        elif kind == "ks":
            ks_all().wait_recv()
            for d in range(1, half):
                kf_copy(lax.rem(s + n - 2 * d, n)).start()
        elif kind == "in":
            send_in(l, 0)

    def act_all(zz, acts):
        for a in acts:
            act(zz, *a[2:])

    for zz, (before, _) in enumerate(plans):
        @pl.when(z == zz)
        def _(zz=zz, before=before):
            act_all(zz, [a for a in before if not a[0]])

    lax.fori_loop(1, n, turn, 0)
    x[:, pl.ds(s, 1)] = turned(0)[:, None]
    in_copy(0, n - 1).start()

    for zz, (before, _) in enumerate(plans):
        @pl.when(z == zz)
        def _(zz=zz, before=before):
            act_all(zz, [a for a in before if a[0]])

    def sib_arrive(l):
        @pl.when(z != l)
        def _():
            sib_wait(l)

    def load(c):
        v = x[c]
        if rows % 16:
            v = v.astype(F32)
        return v.reshape(radix, radix).astype(BF16)

    def store(c, v):
        x[c] = v.reshape(n, rows, radix).astype(BF16)

    total = scales.shape[2]
    first_channel = (z * n + s) * channels

    def prepare(l, _):
        for i in range(2):
            full = kk[:, l, i].astype(F32).reshape(radix, radix)
            kt[l, i] = full.T
        pick = lax.broadcasted_iota(jnp.int32, (channels, total), 1) == (
            lax.broadcasted_iota(jnp.int32, (channels, total), 0) + first_channel
        )
        for i, values in enumerate((scales[l], biases[l])):
            col = jnp.sum(jnp.where(pick, values, 0.0), axis=1, keepdims=True)
            wide = jnp.broadcast_to(0.5 * col, (channels, radix))
            gv[l, i] = wide.reshape(channels, 1, radix)
        return 0

    def compute(l, g):
        ids = [g * group + i for i in range(group)]
        f = [w[0, l, r] for r in range(maps)]
        h = [w[1, l, r] for r in range(maps)]
        u = [load(c) for c in ids]
        y = [dot(v, f[0], NT).astype(BF16) for v in u]
        y = [(dot(h[0], v, NN) * kt[l, 0]).astype(BF16) for v in y]
        y = [dot(f[1], v, NN).astype(BF16) for v in y]
        gate = [0.5 + 0.5 * jnp.tanh(gv[l, 0, c] * v.astype(F32) + gv[l, 1, c]) for c, v in zip(ids, u)]
        y = [(dot(v, h[1], NT) * q).astype(BF16) for v, q in zip(y, gate)]
        y = [dot(v, f[2], NT).astype(BF16) for v in y]
        y = [(dot(h[2], v, NN) * kt[l, 1]).astype(BF16) for v in y]
        y = [dot(f[3], v, NN).astype(BF16) for v in y]
        for c, v, base in zip(ids, y, u):
            store(c, base.astype(F32) + dot(v, h[3], NT))

    kf_all().wait_recv()
    lax.fori_loop(0, layers, prepare, 0)

    def step(l, g):
        @pl.when(l == 0)
        def _():
            in_wait(g)

        compute(l, g)

        @pl.when(l == layers - 1)
        def _():
            def leave(d, _):
                out_copy(g, d).start()
                return 0

            lax.fori_loop(1, n, leave, 0)
            here = pl.ds(g * group, group)
            pltpu.make_async_copy(x.at[here, s], out.at[s, here], out_own).start()

    opens = [min(t for t, (k, _) in enumerate(order) if k == l) for l in range(layers)]

    def turn_step(t, _):
        l = sum(jnp.where(t == i, v[0], 0) for i, v in enumerate(order))
        g = sum(jnp.where(t == i, v[1], 0) for i, v in enumerate(order))
        for zz, (_, slots) in enumerate(plans):
            @pl.when(z == zz)
            def _(zz=zz, slots=slots):
                for tt, acts in slots.items():
                    @pl.when(t == tt)
                    def _(acts=acts):
                        act_all(zz, acts)

        first = sum(jnp.where(t == i, 1, 0) for i in opens)

        @pl.when(first == 1)
        def _():
            sib_arrive(l)

        step(l, g)
        return 0

    lax.fori_loop(0, len(order), turn_step, 0)

    for c in kz_all():
        c.wait_send()
    ks_all().wait_send()
    kf_all().wait_send()
    v = x_in.at[pl.ds(0, n - 1)]
    remote(v, v, in_send, in_recv.at[0], seq=sib).wait_send()

    def sent(count):
        while count:
            some = max(k for k in (1, maps, maps * layers) if k <= count)
            v = w.at[0, 0, 0] if some == 1 else (w.at[0, 0] if some == maps else w.at[0])
            remote(v, v, w_send, z_recv.at[0, 0], seq=sib).wait_send()
            count -= some

    for zz, (before, slots) in enumerate(plans):
        @pl.when(z == zz)
        def _(zz=zz, acts=before + sum(slots.values(), [])):
            count = 0
            for _, _, kind, l, q, up in acts:
                count += kind in ("own", "line", "other")
                count += kind == "line" and onward(zz, l, q, up)
                count += kind == "line" and halved(l, zz, split)
            sent(count)

    v = x.at[:, pl.ds(0, n - 1)]
    remote(v, v, out_send, out_recv, seq=sib).wait_send()
    pltpu.make_async_copy(x.at[:, s], out.at[s], out_own).wait()
    v = out.at[pl.ds(0, n - 1)]
    remote(v, v, out_send, out_recv, seq=sib).wait_recv()


def solution(mesh):
    n, nz = mesh.shape["seq"], mesh.shape["segment"]

    def local(sequence, first, second, kernels, scale, bias):
        rows, local_channels, radix = sequence.shape
        channels = local_channels // n
        group = min(4, channels)
        groups = channels // group
        maps = first.shape[1]
        layers = nz
        total = scale.shape[1]
        x_in = sequence.reshape(rows, n, channels, radix)
        sem = pltpu.SemaphoreType.DMA
        anywhere = pl.BlockSpec(memory_space=pl.ANY)
        result = pl.pallas_call(
            functools.partial(kernel, n, nz, group),
            out_shape=jax.ShapeDtypeStruct((n, channels, rows, radix), BF16),
            in_specs=[anywhere] * 6,
            out_specs=anywhere,
            scratch_shapes=[
                pltpu.VMEM((n, rows, channels, radix), BF16),
                pltpu.VMEM((n, channels, rows, radix), BF16),
                pltpu.VMEM((channels, n, rows, radix), BF16),
                pltpu.VMEM((2, layers, maps, radix, radix), BF16),
                pltpu.VMEM((n, layers, 2, rows, radix), BF16),
                pltpu.VMEM((layers, 1, total), F32),
                pltpu.VMEM((layers, 1, total), F32),
                pltpu.VMEM((layers, 2, radix, radix), F32),
                pltpu.VMEM((layers, 2, channels, 1, radix), F32),
                sem((5,)),
                sem((n,)),
                sem(()),
                sem((groups,)),
                sem(()),
                sem(()),
                sem(()),
                sem(()),
                sem((layers, maps)),
                sem((layers,)),
                sem((3,)),
                sem((3,)),
                sem(()),
                sem(()),
                sem(()),
                sem(()),
            ],
            compiler_params=pltpu.CompilerParams(
                collective_id=0, has_side_effects=True, vmem_limit_bytes=56 * 2**20
            ),
        )(x_in, first, second, kernels, scale, bias)
        return result.reshape(local_channels, rows, radix).transpose(1, 0, 2)

    placed = (
        P("seq", "segment", None),
        P("segment", None, None, None),
        P("segment", None, None, None),
        P("segment", None, "seq", None),
        P("segment", None),
        P("segment", None),
    )
    return jax.shard_map(
        local, mesh=mesh, in_specs=placed, out_specs=P("seq", "segment", None), check_vma=False
    )
```

```python
import functools

import jax
import jax.numpy as jnp
from jax import lax
from jax.experimental import pallas as pl
from jax.experimental.pallas import tpu as pltpu
from jax.sharding import PartitionSpec as P

F32, BF16 = jnp.float32, jnp.bfloat16
NT = (((1,), (1,)), ((), ()))
NN = (((1,), (0,)), ((), ()))


def dot(a, b, dims):
    return lax.dot_general(a, b, dims, preferred_element_type=F32)


T0, WIRE, HOP, STEP, KZ, KS, READY = 5.0, 2.85, 1.4, 1.8, 7.5, 15.5, 18.0


def halved(l, z, j, split):
    return split and not (j > 0 and (abs(l - z) == 1 or (z == 0 and l == 2)))


def pieces(l, z, maps, split):
    pairs = range(maps // 2)
    if not split:
        return [(j, own) for j in pairs for own in (True, False)]
    return [(j, True) for j in pairs] + [(j, False) for j in pairs if not halved(l, z, j, split)]


def line_arrivals(nz, maps, split):
    arrive = [dict() for _ in range(nz)]
    sends = [[] for _ in range(nz)]
    for up in (True, False):
        path = range(nz - 1) if up else range(nz - 1, 0, -1)
        for z in path:
            to = z + 1 if up else z - 1
            own = pieces(z, to, maps, split)
            lead = len(own) if not up or z == 0 else min(1 if z == 1 else 2, len(own))
            free, queue = T0, [(T0, z, q) for q in own[:lead]]
            below = range(z) if up else range(z + 1, nz)
            relays = sorted((arrive[z][l, q], l, q) for l in below for q in pieces(l, to, maps, split))
            queue += relays
            last = relays[-1][0] if relays else T0
            queue += [(last, z, q) for q in own[lead:]]
            for at, l, q in queue:
                free = max(free, at) + WIRE
                arrive[to][l, q] = free + HOP
                if l == z:
                    sends[z].append((0.0 if at == T0 else at, l, q, up))
    return arrive, sends


def passes(l, q, z, nz, maps, split):
    to = z + 1 if l < z else z - 1
    return l != z and 0 <= to < nz and q in pieces(l, to, maps, split)


def transfers(z, arrive, sends, nz, maps, groups, parts, split):
    acts, spread = [], 0
    rising = max([at for (l, q), at in arrive.items() if l < z and passes(l, q, z, nz, maps, split)], default=0.0) - 1.15
    for (l, q), at in sorted(arrive.items(), key=lambda v: v[1]):
        acts.append((at - (1.2 if passes(l, q, z, nz, maps, split) else 0.0), 1, "line", l, q, l < z))
        if q[1] and halved(l, z, q[0], split):
            acts.append((max(at + 4.5, 17.0 + 1.5 * min(spread, 2), rising), 2, "other", l, q, l < z))
            spread += 1
    for at, l, q, up in sends:
        acts.append((at - 1.19 if at else 0.0, 3 if at else 0, "own", l, q, up))
    acts.append((KZ, 4, "kz", 0, (0, True), True))
    acts.append((KS, 4, "ks", 0, (0, True), True))
    at = 13.5 if z == nz - 1 else 15.5
    for g in range(1, groups):
        if z == 0 and g == groups - 1:
            at = max([at] + [v + 0.1 for (l, q), v in arrive.items() if q[1] and halved(l, z, q[0], split)])
        for part in range(parts):
            acts.append((at, 5, "in", g, (part, True), True))
            at = max(at + 6.0 / parts, 21.0 if z == nz - 1 else 0.0)
    return sorted(acts, key=lambda a: a[:2])


def schedule(nz, maps, groups, parts, split):
    arrive, sends = line_arrivals(nz, maps, split)
    plans = []
    for z in range(nz):
        acts = transfers(z, arrive[z], sends[z], nz, maps, groups, parts, split)
        before = [a for a in acts if a[0] <= READY]
        rest = [a for a in acts if a[0] > READY]
        now, slots, order = READY, {}, []
        done = [0] * groups
        x_at = [0.0] + [a[0] + 5.0 for a in acts if a[2] == "in" and a[4][0] == parts - 1]
        opened = set()
        while len(order) < nz * groups:
            t = len(order)
            while rest and rest[0][0] <= now + 0.3:
                slots.setdefault(t, []).append(rest.pop(0))
            held = {a[3] for a in rest if a[2] in ("line", "other")}
            can = [g for g in range(groups) if done[g] < nz and done[g] not in held and (done[g] or x_at[g] <= now)]
            if not can:
                now = min([a[0] for a in rest[:1]] + [x for g, x in enumerate(x_at) if not done[g] and x > now])
                continue
            g = min(can, key=lambda v: (done[v] < 2 and min(done) < 2 and v > 1, v))
            order.append((done[g], g, done[g] not in opened))
            opened.add(done[g])
            done[g] += 1
            now += STEP
        slots.setdefault(len(order) - 1, [])
        slots[len(order) - 1] += rest
        plans.append((before, slots, order))
    return plans


def packed(order, layers, groups):
    base = 2 * layers * groups
    per = 1
    while base ** (per + 1) < 2**30:
        per += 1
    digits = [(l * groups + g) * 2 + int(new) for l, g, new in order]
    chunks = [digits[i : i + per] for i in range(0, len(digits), per)]
    return base, per, [sum(d * base**i for i, d in enumerate(c)) for c in chunks]


def kernel(
    n, nz, group, seq_in, f_own, g_own, k_own, scale_own, bias_own, out,
    raw, x_in, x, w, kk, scales, biases, kt, gv,
    own_sem, raw_sem, in_send, in_recv, out_send, out_recv, out_own,
    w_send, z_recv, sib_recv, kz_send, kz_recv, ks_send, ks_recv, kf_send, kf_recv,
):
    s, z = lax.axis_index("seq"), lax.axis_index("segment")
    core = lax.rem(s, 2)
    sib = s + 1 - 2 * core
    channels, _, rows, radix = x.shape
    groups = channels // group
    maps = w.shape[2]
    layers = w.shape[1]
    half = n // 2
    split = n == 8 and maps % 2 == 0 and nz > 2
    parity = lax.rem(lax.div(s, 2) + lax.div(s, 4), 2) if split else 0
    beside = (s + 2 - 4 * lax.rem(lax.div(s, 2), 2), s + 4 - 8 * lax.rem(lax.div(s, 4), 2))
    parts = 2 if group % 2 == 0 else 1
    plans = schedule(nz, maps, groups, parts, split)

    def peer(d):
        return lax.rem(s + d, n)

    def remote(src, dst, send, recv, **where):
        return pltpu.make_async_remote_copy(
            src_ref=src, dst_ref=dst, send_sem=send, recv_sem=recv,
            device_id=where, device_id_type=pl.DeviceIdType.MESH,
        )

    def in_copy(g, d, part=0, parts=1):
        t = peer(d)
        size = group // parts
        here = pl.ds(g * group + part * size, size)
        return remote(x_in.at[t, here], x.at[here, s], in_send, in_recv.at[g], seq=t)

    def out_copy(c, size, d):
        t = peer(d)
        here = pl.ds(c, size)
        return remote(x.at[here, t], out.at[s, here], out_send, out_recv, seq=t)

    def z_copy(l, i, up):
        v = w.at[core, l, i]
        return remote(v, v, w_send, z_recv.at[l, i], segment=z + 1 if up else z - 1)

    def ex_copy(l, i, j):
        v = w.at[core, l, i]
        return remote(v, v, w_send, z_recv.at[l, i], seq=jnp.where(lax.rem(core + j, 2) == 0, beside[0], beside[1]))

    def sib_copy(l, r):
        v = w.at[core, l, r]
        return remote(v, v, w_send, sib_recv.at[l], seq=sib)

    def sib_wait(l):
        v = w.at[1 - core, l]
        remote(v, v, w_send, sib_recv.at[l], seq=sib).wait_recv()

    def kz_copy(d, l):
        to = lax.rem(z + d, nz)
        return tuple(
            remote(v, v, kz_send.at[i], kz_recv.at[i], segment=to)
            for i, v in enumerate((kk.at[s, l], scales.at[l], biases.at[l]))
        )

    def kz_all():
        others = pl.ds(0, nz - 1)
        return tuple(
            remote(v, v, kz_send.at[i], kz_recv.at[i], segment=lax.rem(z + 1, nz))
            for i, v in enumerate((kk.at[s, others], scales.at[others], biases.at[others]))
        )

    def ks_copy(d, owner):
        v = kk.at[owner]
        return remote(v, v, ks_send, ks_recv, seq=lax.rem(s + 2 * d, n))

    def ks_all():
        v = kk.at[pl.ds(0, half - 1)]
        return remote(v, v, ks_send, ks_recv, seq=sib)

    def kf_copy(owner):
        v = kk.at[owner]
        return remote(v, v, kf_send, kf_recv, seq=sib)

    def kf_all():
        v = kk.at[pl.ds(0, half)]
        return remote(v, v, kf_send, kf_recv, seq=sib)

    def in_wait(g):
        v = x.at[pl.ds(g * group, group), pl.ds(0, n - 1)]
        remote(v, v, in_send, in_recv.at[g], seq=sib).wait_recv()

    own = [
        pltpu.make_async_copy(f_own.at[0], w.at[0, z], own_sem.at[0]),
        pltpu.make_async_copy(g_own.at[0], w.at[1, z], own_sem.at[1]),
        pltpu.make_async_copy(k_own.at[0], kk.at[s, z], own_sem.at[2]),
        pltpu.make_async_copy(scale_own, scales.at[z], own_sem.at[3]),
        pltpu.make_async_copy(bias_own, biases.at[z], own_sem.at[4]),
    ]
    def raw_copy(d):
        t = peer(d)
        return pltpu.make_async_copy(seq_in.at[:, t], raw.at[t], raw_sem.at[d])

    for c in own:
        c.start()
    for d in range(1, n + 1):
        raw_copy(d % n).start()

    barrier = pltpu.get_barrier_semaphore()
    mesh_id = pl.DeviceIdType.MESH

    def greet(d, _):
        pl.semaphore_signal(barrier, inc=1, device_id={"seq": peer(d)}, device_id_type=mesh_id)
        return 0

    lax.fori_loop(1, n, greet, 0)

    def greet_z(d, _):
        to = lax.rem(z + d, nz)
        pl.semaphore_signal(barrier, inc=1, device_id={"segment": to}, device_id_type=mesh_id)
        return 0

    lax.fori_loop(1, nz, greet_z, 0)
    pl.semaphore_wait(barrier, n + nz - 2)

    for c in own:
        c.wait()

    for d in range(1, nz):
        for c in kz_copy(d, z):
            c.start()

    def send_in(g, part):
        def one(d, _):
            in_copy(g, d, part, parts).start()
            return 0

        lax.fori_loop(1, n, one, 0)

    def turned(d):
        raw_copy(d).wait()
        v = raw[peer(d)]
        return jnp.swapaxes(v, 0, 1)

    def turn(d, _):
        x_in[peer(d)] = turned(d)

        @pl.when(d > 1)
        def _():
            in_copy(0, d - 1).start()

        return 0

    def mine(q):
        return 2 * q[0] + (parity if q[1] else 1 - parity)

    def act(zz, kind, l, q, up):
        if kind == "own":
            z_copy(l, mine(q), up).start()
        elif kind == "line":
            i = mine(q)
            c = z_copy(l, i, up)
            c.wait_recv()
            if passes(l, q, zz, nz, maps, split):
                c.start()
            if q[1] and halved(l, zz, q[0], split):
                ex_copy(l, i, q[0]).start()
            sib_copy(l, i).start()
        elif kind == "other":
            i = 2 * q[0] + 1 - parity
            ex_copy(l, i, q[0]).wait_recv()
            sib_copy(l, i).start()
        elif kind == "kz":
            for c in kz_all():
                c.wait_recv()
            for d in range(1, half):
                ks_copy(d, s).start()
            kf_copy(s).start()
        elif kind == "ks":
            ks_all().wait_recv()
            for d in range(1, half):
                kf_copy(lax.rem(s + n - 2 * d, n)).start()
        elif kind == "in":
            send_in(l, q[0])

    def act_all(zz, acts):
        for a in acts:
            act(zz, *a[2:])

    for zz, (before, _, _) in enumerate(plans):
        @pl.when(z == zz)
        def _(zz=zz, before=before):
            act_all(zz, [a for a in before if not a[0]])

    lax.fori_loop(1, n, turn, 0)
    x[:, pl.ds(s, 1)] = turned(0)[:, None]
    in_copy(0, n - 1).start()

    for zz, (before, _, _) in enumerate(plans):
        @pl.when(z == zz)
        def _(zz=zz, before=before):
            act_all(zz, [a for a in before if a[0]])

    def sib_arrive(l):
        @pl.when(z != l)
        def _():
            sib_wait(l)

    def load(c):
        v = x[c]
        if rows % 16:
            v = v.astype(F32)
        return v.reshape(radix, radix).astype(BF16)

    def store(c, v):
        x[c] = v.reshape(n, rows, radix).astype(BF16)

    total = scales.shape[2]
    first_channel = (z * n + s) * channels

    def prepare(l, _):
        for i in range(2):
            full = kk[:, l, i].astype(F32).reshape(radix, radix)
            kt[l, i] = full.T
        pick = lax.broadcasted_iota(jnp.int32, (channels, total), 1) == (
            lax.broadcasted_iota(jnp.int32, (channels, total), 0) + first_channel
        )
        for i, values in enumerate((scales[l], biases[l])):
            col = jnp.sum(jnp.where(pick, values, 0.0), axis=1, keepdims=True)
            wide = jnp.broadcast_to(0.5 * col, (channels, radix))
            gv[l, i] = wide.reshape(channels, 1, radix)
        return 0

    def compute(l, c, size):
        ids = [c + i for i in range(size)]
        f = [w[0, l, r] for r in range(maps)]
        h = [w[1, l, r] for r in range(maps)]
        u = [load(c) for c in ids]
        y = [dot(v, f[0], NT).astype(BF16) for v in u]
        y = [(dot(h[0], v, NN) * kt[l, 0]).astype(BF16) for v in y]
        y = [dot(f[1], v, NN).astype(BF16) for v in y]
        gate = [0.5 + 0.5 * jnp.tanh(gv[l, 0, c] * v.astype(F32) + gv[l, 1, c]) for c, v in zip(ids, u)]
        y = [(dot(v, h[1], NT) * q).astype(BF16) for v, q in zip(y, gate)]
        y = [dot(v, f[2], NT).astype(BF16) for v in y]
        y = [(dot(h[2], v, NN) * kt[l, 1]).astype(BF16) for v in y]
        y = [dot(f[3], v, NN).astype(BF16) for v in y]
        for c, v, base in zip(ids, y, u):
            store(c, base.astype(F32) + dot(v, h[3], NT))

    kf_all().wait_recv()
    lax.fori_loop(0, layers, prepare, 0)

    def step(l, g, c, size, opening):
        @pl.when(opening)
        def _():
            in_wait(g)

        compute(l, c, size)

        @pl.when(l == layers - 1)
        def _():
            def leave(d, _):
                out_copy(c, size, d).start()
                return 0

            lax.fori_loop(1, n, leave, 0)
            here = pl.ds(c, size)
            pltpu.make_async_copy(x.at[here, s], out.at[s, here], out_own).start()

    codes = [packed(order, layers, groups) for _, _, order in plans]
    base, per = codes[0][:2]
    steps = layers * groups

    def turn_step(t, code):
        digit = lax.rem(code, base)
        l, g = lax.div(digit, 2 * groups), lax.rem(lax.div(digit, 2), groups)
        for zz, (_, slots, _) in enumerate(plans):
            @pl.when(z == zz)
            def _(zz=zz, slots=slots):
                for tt, acts in slots.items():
                    @pl.when(t == tt)
                    def _(acts=acts):
                        act_all(zz, acts)

        @pl.when(lax.rem(digit, 2) == 1)
        def _():
            sib_arrive(l)

        step(l, g, g * group, group, l == 0)
        return lax.div(code, base)

    def run(k, _):
        code = 0
        for zz in range(nz):
            for kk_, value in enumerate(codes[zz][2]):
                code += jnp.where(jnp.logical_and(z == zz, k == kk_), value, 0)
        lax.fori_loop(k * per, jnp.minimum(k * per + per, steps), turn_step, code)
        return 0

    lax.fori_loop(0, len(codes[0][2]), run, 0)

    for c in kz_all():
        c.wait_send()
    ks_all().wait_send()
    kf_all().wait_send()
    v = x_in.at[pl.ds(0, n - 1)]
    remote(v, v, in_send, in_recv.at[0], seq=sib).wait_send()

    def sent(count):
        while count:
            some = max(k for k in (1, maps, maps * layers) if k <= count)
            v = w.at[0, 0, 0] if some == 1 else (w.at[0, 0] if some == maps else w.at[0])
            remote(v, v, w_send, z_recv.at[0, 0], seq=sib).wait_send()
            count -= some

    for zz, (before, slots, _) in enumerate(plans):
        @pl.when(z == zz)
        def _(zz=zz, acts=before + sum(slots.values(), [])):
            count = 0
            for _, _, kind, l, q, up in acts:
                count += kind in ("own", "line", "other")
                count += kind == "line" and passes(l, q, zz, nz, maps, split)
                count += kind == "line" and q[1] and halved(l, zz, q[0], split)
            sent(count)

    v = x.at[:, pl.ds(0, n - 1)]
    remote(v, v, out_send, out_recv, seq=sib).wait_send()
    pltpu.make_async_copy(x.at[:, s], out.at[s], out_own).wait()
    v = out.at[pl.ds(0, n - 1)]
    remote(v, v, out_send, out_recv, seq=sib).wait_recv()


def turn_kernel(v, out, gone, save):
    n, width = v.shape[:2]

    def put(t):
        here = pl.ds(t * width, width)
        return pltpu.make_async_copy(gone.at[t], out.at[:, here], save.at[t])

    def one(t, _):
        gone[t] = jnp.swapaxes(v[t], 0, 1)
        put(t).start()
        return 0

    lax.fori_loop(0, n, one, 0)
    for t in range(n):
        put(t).wait()


def solution(mesh):
    n, nz = mesh.shape["seq"], mesh.shape["segment"]

    def local(sequence, first, second, kernels, scale, bias):
        rows, local_channels, radix = sequence.shape
        channels = local_channels // n
        group = min(4, channels)
        groups = channels // group
        maps = first.shape[1]
        layers = nz
        total = scale.shape[1]
        x_in = sequence.reshape(rows, n, channels, radix)
        sem = pltpu.SemaphoreType.DMA
        anywhere = pl.BlockSpec(memory_space=pl.ANY)
        result = pl.pallas_call(
            functools.partial(kernel, n, nz, group),
            out_shape=pltpu.VMEM((n, channels, rows, radix), BF16),
            in_specs=[anywhere] * 6,
            out_specs=anywhere,
            scratch_shapes=[
                pltpu.VMEM((n, rows, channels, radix), BF16),
                pltpu.VMEM((n, channels, rows, radix), BF16),
                pltpu.VMEM((channels, n, rows, radix), BF16),
                pltpu.VMEM((2, layers, maps, radix, radix), BF16),
                pltpu.VMEM((n, layers, 2, rows, radix), BF16),
                pltpu.VMEM((layers, 1, total), F32),
                pltpu.VMEM((layers, 1, total), F32),
                pltpu.VMEM((layers, 2, radix, radix), F32),
                pltpu.VMEM((layers, 2, channels, 1, radix), F32),
                sem((5,)),
                sem((n,)),
                sem(()),
                sem((groups,)),
                sem(()),
                sem(()),
                sem(()),
                sem(()),
                sem((layers, maps)),
                sem((layers,)),
                sem((3,)),
                sem((3,)),
                sem(()),
                sem(()),
                sem(()),
                sem(()),
            ],
            compiler_params=pltpu.CompilerParams(
                collective_id=0, has_side_effects=True, vmem_limit_bytes=56 * 2**20
            ),
        )(x_in, first, second, kernels, scale, bias)
        return pl.pallas_call(
            turn_kernel,
            out_shape=jax.ShapeDtypeStruct((rows, local_channels, radix), BF16),
            in_specs=[pl.BlockSpec(memory_space=pltpu.VMEM)],
            out_specs=anywhere,
            scratch_shapes=[pltpu.VMEM((n, rows, channels, radix), BF16), sem((n,))],
        )(pltpu.with_memory_space_constraint(result, pltpu.VMEM))

    placed = (
        P("seq", "segment", None),
        P("segment", None, None, None),
        P("segment", None, None, None),
        P("segment", None, "seq", None),
        P("segment", None),
        P("segment", None),
    )
    return jax.shard_map(
        local, mesh=mesh, in_specs=placed, out_specs=P("seq", "segment", None), check_vma=False
    )
```

```python
import functools

import jax
import jax.numpy as jnp
from jax import lax
from jax.experimental import pallas as pl
from jax.experimental.pallas import tpu as pltpu
from jax.sharding import PartitionSpec as P

F32, BF16 = jnp.float32, jnp.bfloat16
NT = (((1,), (1,)), ((), ()))
NN = (((1,), (0,)), ((), ()))


def dot(a, b, dims):
    return lax.dot_general(a, b, dims, preferred_element_type=F32)


T0, WIRE, HOP, STEP, KZ, KS, READY = 5.0, 2.85, 1.4, 1.8, 7.5, 15.5, 18.0


def halved(l, z, j, split):
    return split and not (j > 0 and (abs(l - z) == 1 or (z == 0 and l == 2)))


def pieces(l, z, maps, split):
    pairs = range(maps // 2)
    if not split:
        return [(j, own) for j in pairs for own in (True, False)]
    return [(j, True) for j in pairs] + [(j, False) for j in pairs if not halved(l, z, j, split)]


def line_arrivals(nz, maps, split):
    arrive = [dict() for _ in range(nz)]
    sends = [[] for _ in range(nz)]
    for up in (True, False):
        path = range(nz - 1) if up else range(nz - 1, 0, -1)
        for z in path:
            to = z + 1 if up else z - 1
            own = pieces(z, to, maps, split)
            lead = len(own) if not up or z == 0 else 1
            free, queue = (T0 if z or not up else T0 - 1.6), [(T0, z, q) for q in own[:lead]]
            below = range(z) if up else range(z + 1, nz)
            relays = sorted((arrive[z][l, q], l, q) for l in below for q in pieces(l, to, maps, split))
            queue += relays
            last = relays[-1][0] if relays else T0
            queue += [(last, z, q) for q in own[lead:]]
            for at, l, q in queue:
                free = max(free, at) + WIRE
                arrive[to][l, q] = free + HOP
                if l == z:
                    sends[z].append((0.0 if at == T0 else at, l, q, up))
    return arrive, sends


def passes(l, q, z, nz, maps, split):
    to = z + 1 if l < z else z - 1
    return l != z and 0 <= to < nz and q in pieces(l, to, maps, split)


def transfers(z, arrive, sends, nz, maps, groups, parts, split):
    acts, spread = [], 0
    rising = max([at for (l, q), at in arrive.items() if l < z and passes(l, q, z, nz, maps, split)], default=0.0) - 1.15
    for (l, q), at in sorted(arrive.items(), key=lambda v: v[1]):
        acts.append((at - (1.2 if passes(l, q, z, nz, maps, split) else 0.0), 1, "line", l, q, l < z))
        if q[1] and halved(l, z, q[0], split):
            acts.append((max(at + (3.0 if z == 0 and l == nz - 1 else 4.5), 17.0 + 1.5 * min(spread, 2), rising), 2, "other", l, q, l < z))
            spread += 1
    for at, l, q, up in sends:
        acts.append((at - 1.19 if at else 0.0, 3 if at else 0, "own", l, q, up))
    acts.append((KZ if z in (0, nz - 1) else KZ + 4.0, 4, "kz", 0, (0, True), True))
    acts.append((KS if z in (0, nz - 1) else KS + 2.4, 4, "ks", 0, (0, True), True))
    swaps = [v for (l, q), v in arrive.items() if q[1] and halved(l, z, q[0], split)]
    entries = [(g, part) for g in range(1, groups) for part in range(parts)]
    if z == nz - 1:
        first, then, gap = [13.5, 17.9], 25.3, 1.0
    elif z == 0:
        first, then, gap = [15.5, 18.5, 21.5, 24.5], max(swaps, default=0.0) + 0.1, 0.1
    else:
        first, then, gap = [15.5, 17.0], 19.5, 3.0
    for i, (g, part) in enumerate(entries):
        at = first[i] if i < len(first) else then + gap * (i - len(first))
        acts.append((at, 5, "in", g, (part, True), True))
    return sorted(acts, key=lambda a: a[:2])


def schedule(nz, maps, groups, parts, split):
    arrive, sends = line_arrivals(nz, maps, split)
    plans = []
    for z in range(nz):
        acts = transfers(z, arrive[z], sends[z], nz, maps, groups, parts, split)
        before = [a for a in acts if a[0] <= READY]
        rest = [a for a in acts if a[0] > READY]
        now, slots, order = READY, {}, []
        done = [0] * groups
        x_at = [0.0] + [a[0] + 5.0 for a in acts if a[2] == "in" and a[4][0] == parts - 1]
        opened = set()
        while len(order) < nz * groups:
            t = len(order)
            while rest and rest[0][0] <= now + 0.3:
                slots.setdefault(t, []).append(rest.pop(0))
            held = {a[3] for a in rest if a[2] in ("line", "other")}
            can = [g for g in range(groups) if done[g] < nz and done[g] not in held and (done[g] or x_at[g] <= now)]
            if not can:
                now = min([a[0] for a in rest[:1]] + [x for g, x in enumerate(x_at) if not done[g] and x > now])
                continue
            if z == nz - 1:
                g = min(can, key=lambda v: (v > 1 or done[v] > 1, v))
            else:
                g = min(can, key=lambda v: (done[v] < 2 and min(done) < 2 and v > 1, v))
            order.append((done[g], g, done[g] not in opened))
            opened.add(done[g])
            done[g] += 1
            now += STEP
        slots.setdefault(len(order) - 1, [])
        slots[len(order) - 1] += rest
        plans.append((before, slots, order))
    return plans


def packed(order, layers, groups):
    base = 2 * layers * groups
    per = 1
    while base ** (per + 1) < 2**30:
        per += 1
    digits = [(l * groups + g) * 2 + int(new) for l, g, new in order]
    chunks = [digits[i : i + per] for i in range(0, len(digits), per)]
    return base, per, [sum(d * base**i for i, d in enumerate(c)) for c in chunks]


def kernel(
    n, nz, group, seq_in, f_own, g_own, k_own, scale_own, bias_own, out,
    raw, x_in, x, w, kk, scales, biases, kt, gv,
    own_sem, raw_sem, in_send, in_recv, out_send, out_recv, out_own,
    w_send, z_recv, sib_recv, kz_send, kz_recv, ks_send, ks_recv, kf_send, kf_recv,
):
    s, z = lax.axis_index("seq"), lax.axis_index("segment")
    core = lax.rem(s, 2)
    sib = s + 1 - 2 * core
    channels, _, rows, radix = x.shape
    groups = channels // group
    maps = w.shape[2]
    layers = w.shape[1]
    half = n // 2
    split = n == 8 and maps % 2 == 0 and nz > 2
    parity = lax.rem(lax.div(s, 2) + lax.div(s, 4), 2) if split else 0
    beside = (s + 2 - 4 * lax.rem(lax.div(s, 2), 2), s + 4 - 8 * lax.rem(lax.div(s, 4), 2))
    parts = 2 if group % 2 == 0 else 1
    plans = schedule(nz, maps, groups, parts, split)

    def peer(d):
        return lax.rem(s + d, n)

    def remote(src, dst, send, recv, **where):
        return pltpu.make_async_remote_copy(
            src_ref=src, dst_ref=dst, send_sem=send, recv_sem=recv,
            device_id=where, device_id_type=pl.DeviceIdType.MESH,
        )

    def in_copy(g, d, part=0, parts=1):
        t = peer(d)
        size = group // parts
        here = pl.ds(g * group + part * size, size)
        return remote(x_in.at[t, here], x.at[here, s], in_send, in_recv.at[g], seq=t)

    def out_copy(c, size, d):
        t = peer(d)
        here = pl.ds(c, size)
        return remote(x.at[here, t], out.at[s, here], out_send, out_recv, seq=t)

    def z_copy(l, i, up):
        v = w.at[core, l, i]
        return remote(v, v, w_send, z_recv.at[l, i], segment=z + 1 if up else z - 1)

    def ex_copy(l, i, j):
        v = w.at[core, l, i]
        return remote(v, v, w_send, z_recv.at[l, i], seq=jnp.where(lax.rem(core + j, 2) == 0, beside[0], beside[1]))

    def sib_copy(l, r):
        v = w.at[core, l, r]
        return remote(v, v, w_send, sib_recv.at[l], seq=sib)

    def sib_wait(l):
        v = w.at[1 - core, l]
        remote(v, v, w_send, sib_recv.at[l], seq=sib).wait_recv()

    def kz_copy(d, l):
        to = lax.rem(z + d, nz)
        return tuple(
            remote(v, v, kz_send.at[i], kz_recv.at[i], segment=to)
            for i, v in enumerate((kk.at[s, l], scales.at[l], biases.at[l]))
        )

    def kz_all():
        others = pl.ds(0, nz - 1)
        return tuple(
            remote(v, v, kz_send.at[i], kz_recv.at[i], segment=lax.rem(z + 1, nz))
            for i, v in enumerate((kk.at[s, others], scales.at[others], biases.at[others]))
        )

    def ks_copy(d, owner):
        v = kk.at[owner]
        return remote(v, v, ks_send, ks_recv, seq=lax.rem(s + 2 * d, n))

    def ks_all():
        v = kk.at[pl.ds(0, half - 1)]
        return remote(v, v, ks_send, ks_recv, seq=sib)

    def kf_copy(owner):
        v = kk.at[owner]
        return remote(v, v, kf_send, kf_recv, seq=sib)

    def kf_all():
        v = kk.at[pl.ds(0, half)]
        return remote(v, v, kf_send, kf_recv, seq=sib)

    def in_wait(g):
        v = x.at[pl.ds(g * group, group), pl.ds(0, n - 1)]
        remote(v, v, in_send, in_recv.at[g], seq=sib).wait_recv()

    own = [
        pltpu.make_async_copy(f_own.at[0], w.at[0, z], own_sem.at[0]),
        pltpu.make_async_copy(g_own.at[0], w.at[1, z], own_sem.at[1]),
        pltpu.make_async_copy(k_own.at[0], kk.at[s, z], own_sem.at[2]),
        pltpu.make_async_copy(scale_own, scales.at[z], own_sem.at[3]),
        pltpu.make_async_copy(bias_own, biases.at[z], own_sem.at[4]),
    ]
    def raw_copy(d):
        t = peer(d)
        return pltpu.make_async_copy(seq_in.at[:, t], raw.at[t], raw_sem.at[d])

    for c in own:
        c.start()
    for d in range(1, n + 1):
        raw_copy(d % n).start()

    barrier = pltpu.get_barrier_semaphore()
    mesh_id = pl.DeviceIdType.MESH

    def greet(d, _):
        pl.semaphore_signal(barrier, inc=1, device_id={"seq": peer(d)}, device_id_type=mesh_id)
        return 0

    lax.fori_loop(1, n, greet, 0)

    def greet_z(d, _):
        to = lax.rem(z + d, nz)
        pl.semaphore_signal(barrier, inc=1, device_id={"segment": to}, device_id_type=mesh_id)
        return 0

    lax.fori_loop(1, nz, greet_z, 0)
    pl.semaphore_wait(barrier, n + nz - 2)

    for c in own:
        c.wait()

    def give_k(d):
        for c in kz_copy(d, z):
            c.start()

    give_k(nz - 1)

    @pl.when(z > 0)
    def _():
        for d in range(1, nz - 1):
            give_k(d)

    def send_in(g, part):
        def one(d, _):
            in_copy(g, d, part, parts).start()
            return 0

        lax.fori_loop(1, n, one, 0)

    def turned(d):
        raw_copy(d).wait()
        v = raw[peer(d)]
        return jnp.swapaxes(v, 0, 1)

    def turn(d, _):
        x_in[peer(d)] = turned(d)

        @pl.when(d > 1)
        def _():
            in_copy(0, d - 1).start()

        return 0

    def mine(q):
        return 2 * q[0] + (parity if q[1] else 1 - parity)

    def act(zz, kind, l, q, up):
        if kind == "own":
            z_copy(l, mine(q), up).start()
        elif kind == "line":
            i = mine(q)
            c = z_copy(l, i, up)
            c.wait_recv()
            if passes(l, q, zz, nz, maps, split):
                c.start()
            if q[1] and halved(l, zz, q[0], split):
                ex_copy(l, i, q[0]).start()
            sib_copy(l, i).start()
        elif kind == "other":
            i = 2 * q[0] + 1 - parity
            ex_copy(l, i, q[0]).wait_recv()
            sib_copy(l, i).start()
        elif kind == "kz":
            for c in kz_all():
                c.wait_recv()
            for d in range(1, half):
                ks_copy(d, s).start()
            kf_copy(s).start()
        elif kind == "ks":
            ks_all().wait_recv()
            for d in range(1, half):
                kf_copy(lax.rem(s + n - 2 * d, n)).start()
        elif kind == "in":
            send_in(l, q[0])

    def act_all(zz, acts):
        for a in acts:
            act(zz, *a[2:])

    for zz, (before, _, _) in enumerate(plans):
        @pl.when(z == zz)
        def _(zz=zz, before=before):
            now = [a for a in before if not a[0]]
            if zz:
                act_all(zz, now)
            else:
                act_all(zz, [a for a in now if a[4][1]])
                for d in range(nz - 2, 0, -1):
                    give_k(d)
                act_all(zz, [a for a in now if not a[4][1]])

    lax.fori_loop(1, n, turn, 0)
    x[:, pl.ds(s, 1)] = turned(0)[:, None]
    in_copy(0, n - 1).start()

    for zz, (before, _, _) in enumerate(plans):
        @pl.when(z == zz)
        def _(zz=zz, before=before):
            act_all(zz, [a for a in before if a[0]])

    def sib_arrive(l):
        @pl.when(z != l)
        def _():
            sib_wait(l)

    def load(c):
        v = x[c]
        if rows % 16:
            v = v.astype(F32)
        return v.reshape(radix, radix).astype(BF16)

    def store(c, v):
        x[c] = v.reshape(n, rows, radix).astype(BF16)

    total = scales.shape[2]
    first_channel = (z * n + s) * channels

    def prepare(l, _):
        for i in range(2):
            full = kk[:, l, i].astype(F32).reshape(radix, radix)
            kt[l, i] = full.T
        pick = lax.broadcasted_iota(jnp.int32, (channels, total), 1) == (
            lax.broadcasted_iota(jnp.int32, (channels, total), 0) + first_channel
        )
        for i, values in enumerate((scales[l], biases[l])):
            col = jnp.sum(jnp.where(pick, values, 0.0), axis=1, keepdims=True)
            wide = jnp.broadcast_to(0.5 * col, (channels, radix))
            gv[l, i] = wide.reshape(channels, 1, radix)
        return 0

    def compute(l, c, size):
        ids = [c + i for i in range(size)]
        f = [w[0, l, r] for r in range(maps)]
        h = [w[1, l, r] for r in range(maps)]
        u = [load(c) for c in ids]
        y = [dot(v, f[0], NT).astype(BF16) for v in u]
        y = [(dot(h[0], v, NN) * kt[l, 0]).astype(BF16) for v in y]
        y = [dot(f[1], v, NN).astype(BF16) for v in y]
        gate = [0.5 + 0.5 * jnp.tanh(gv[l, 0, c] * v.astype(F32) + gv[l, 1, c]) for c, v in zip(ids, u)]
        y = [(dot(v, h[1], NT) * q).astype(BF16) for v, q in zip(y, gate)]
        y = [dot(v, f[2], NT).astype(BF16) for v in y]
        y = [(dot(h[2], v, NN) * kt[l, 1]).astype(BF16) for v in y]
        y = [dot(f[3], v, NN).astype(BF16) for v in y]
        for c, v, base in zip(ids, y, u):
            store(c, base.astype(F32) + dot(v, h[3], NT))

    kf_all().wait_recv()
    lax.fori_loop(0, layers, prepare, 0)

    def step(l, g, c, size, opening):
        @pl.when(opening)
        def _():
            in_wait(g)

        compute(l, c, size)

        @pl.when(l == layers - 1)
        def _():
            def leave(d, _):
                out_copy(c, size, d).start()
                return 0

            lax.fori_loop(1, n, leave, 0)
            here = pl.ds(c, size)
            pltpu.make_async_copy(x.at[here, s], out.at[s, here], out_own).start()

    codes = [packed(order, layers, groups) for _, _, order in plans]
    base, per = codes[0][:2]
    steps = layers * groups

    def turn_step(t, code):
        digit = lax.rem(code, base)
        l, g = lax.div(digit, 2 * groups), lax.rem(lax.div(digit, 2), groups)
        for zz, (_, slots, _) in enumerate(plans):
            @pl.when(z == zz)
            def _(zz=zz, slots=slots):
                for tt, acts in slots.items():
                    @pl.when(t == tt)
                    def _(acts=acts):
                        act_all(zz, acts)

        @pl.when(lax.rem(digit, 2) == 1)
        def _():
            sib_arrive(l)

        step(l, g, g * group, group, l == 0)
        return lax.div(code, base)

    def run(k, _):
        code = 0
        for zz in range(nz):
            for kk_, value in enumerate(codes[zz][2]):
                code += jnp.where(jnp.logical_and(z == zz, k == kk_), value, 0)
        lax.fori_loop(k * per, jnp.minimum(k * per + per, steps), turn_step, code)
        return 0

    lax.fori_loop(0, len(codes[0][2]), run, 0)

    for c in kz_all():
        c.wait_send()
    ks_all().wait_send()
    kf_all().wait_send()
    v = x_in.at[pl.ds(0, n - 1)]
    remote(v, v, in_send, in_recv.at[0], seq=sib).wait_send()

    def sent(count):
        while count:
            some = max(k for k in (1, maps, maps * layers) if k <= count)
            v = w.at[0, 0, 0] if some == 1 else (w.at[0, 0] if some == maps else w.at[0])
            remote(v, v, w_send, z_recv.at[0, 0], seq=sib).wait_send()
            count -= some

    for zz, (before, slots, _) in enumerate(plans):
        @pl.when(z == zz)
        def _(zz=zz, acts=before + sum(slots.values(), [])):
            count = 0
            for _, _, kind, l, q, up in acts:
                count += kind in ("own", "line", "other")
                count += kind == "line" and passes(l, q, zz, nz, maps, split)
                count += kind == "line" and q[1] and halved(l, zz, q[0], split)
            sent(count)

    v = x.at[:, pl.ds(0, n - 1)]
    remote(v, v, out_send, out_recv, seq=sib).wait_send()
    pltpu.make_async_copy(x.at[:, s], out.at[s], out_own).wait()
    v = out.at[pl.ds(0, n - 1)]
    remote(v, v, out_send, out_recv, seq=sib).wait_recv()


def turn_kernel(v, out, gone, save):
    n, width = v.shape[:2]

    def put(t):
        here = pl.ds(t * width, width)
        return pltpu.make_async_copy(gone.at[t], out.at[:, here], save.at[t])

    def one(t, _):
        gone[t] = jnp.swapaxes(v[t], 0, 1)
        put(t).start()
        return 0

    lax.fori_loop(0, n, one, 0)
    for t in range(n):
        put(t).wait()


def solution(mesh):
    n, nz = mesh.shape["seq"], mesh.shape["segment"]

    def local(sequence, first, second, kernels, scale, bias):
        rows, local_channels, radix = sequence.shape
        channels = local_channels // n
        group = min(4, channels)
        groups = channels // group
        maps = first.shape[1]
        layers = nz
        total = scale.shape[1]
        x_in = sequence.reshape(rows, n, channels, radix)
        sem = pltpu.SemaphoreType.DMA
        anywhere = pl.BlockSpec(memory_space=pl.ANY)
        result = pl.pallas_call(
            functools.partial(kernel, n, nz, group),
            out_shape=pltpu.VMEM((n, channels, rows, radix), BF16),
            in_specs=[anywhere] * 6,
            out_specs=anywhere,
            scratch_shapes=[
                pltpu.VMEM((n, rows, channels, radix), BF16),
                pltpu.VMEM((n, channels, rows, radix), BF16),
                pltpu.VMEM((channels, n, rows, radix), BF16),
                pltpu.VMEM((2, layers, maps, radix, radix), BF16),
                pltpu.VMEM((n, layers, 2, rows, radix), BF16),
                pltpu.VMEM((layers, 1, total), F32),
                pltpu.VMEM((layers, 1, total), F32),
                pltpu.VMEM((layers, 2, radix, radix), F32),
                pltpu.VMEM((layers, 2, channels, 1, radix), F32),
                sem((5,)),
                sem((n,)),
                sem(()),
                sem((groups,)),
                sem(()),
                sem(()),
                sem(()),
                sem(()),
                sem((layers, maps)),
                sem((layers,)),
                sem((3,)),
                sem((3,)),
                sem(()),
                sem(()),
                sem(()),
                sem(()),
            ],
            compiler_params=pltpu.CompilerParams(
                collective_id=0, has_side_effects=True, vmem_limit_bytes=56 * 2**20
            ),
        )(x_in, first, second, kernels, scale, bias)
        return pl.pallas_call(
            turn_kernel,
            out_shape=jax.ShapeDtypeStruct((rows, local_channels, radix), BF16),
            in_specs=[pl.BlockSpec(memory_space=pltpu.VMEM)],
            out_specs=anywhere,
            scratch_shapes=[pltpu.VMEM((n, rows, channels, radix), BF16), sem((n,))],
        )(pltpu.with_memory_space_constraint(result, pltpu.VMEM))

    placed = (
        P("seq", "segment", None),
        P("segment", None, None, None),
        P("segment", None, None, None),
        P("segment", None, "seq", None),
        P("segment", None),
        P("segment", None),
    )
    return jax.shard_map(
        local, mesh=mesh, in_specs=placed, out_specs=P("seq", "segment", None), check_vma=False
    )
```

```python
import functools

import jax
import jax.numpy as jnp
from jax import lax
from jax.experimental import pallas as pl
from jax.experimental.pallas import tpu as pltpu
from jax.sharding import PartitionSpec as P

F32, BF16 = jnp.float32, jnp.bfloat16
NT = (((1,), (1,)), ((), ()))
NN = (((1,), (0,)), ((), ()))


def dot(a, b, dims):
    return lax.dot_general(a, b, dims, preferred_element_type=F32)


T0, WIRE, HOP, STEP, KZ, KS, READY = 5.0, 2.85, 1.4, 1.8, 7.5, 15.5, 18.0


def halved(l, z, j, split):
    return split and not (j > 0 and (abs(l - z) == 1 or (z == 0 and l == 2)))


def pieces(l, z, maps, split):
    pairs = range(maps // 2)
    if not split:
        return [(j, own) for j in pairs for own in (True, False)]
    return [(j, True) for j in pairs] + [(j, False) for j in pairs if not halved(l, z, j, split)]


def line_arrivals(nz, maps, split):
    arrive = [dict() for _ in range(nz)]
    sends = [[] for _ in range(nz)]
    for up in (True, False):
        path = range(nz - 1) if up else range(nz - 1, 0, -1)
        for z in path:
            to = z + 1 if up else z - 1
            own = pieces(z, to, maps, split)
            lead = len(own) if not up or z == 0 else 1
            free, queue = (T0 if z or not up else T0 - 1.6), [(T0, z, q) for q in own[:lead]]
            below = range(z) if up else range(z + 1, nz)
            relays = sorted((arrive[z][l, q], l, q) for l in below for q in pieces(l, to, maps, split))
            queue += relays
            last = relays[-1][0] if relays else T0
            queue += [(last, z, q) for q in own[lead:]]
            for at, l, q in queue:
                free = max(free, at) + WIRE
                arrive[to][l, q] = free + HOP
                if l == z:
                    sends[z].append((0.0 if at == T0 else at, l, q, up))
    return arrive, sends


def passes(l, q, z, nz, maps, split):
    to = z + 1 if l < z else z - 1
    return l != z and 0 <= to < nz and q in pieces(l, to, maps, split)


def transfers(z, arrive, sends, nz, maps, groups, parts, split):
    acts, spread = [], 0
    rising = max([at for (l, q), at in arrive.items() if l < z and passes(l, q, z, nz, maps, split)], default=0.0) - 1.15
    for (l, q), at in sorted(arrive.items(), key=lambda v: v[1]):
        acts.append((at - (1.2 if passes(l, q, z, nz, maps, split) else 0.0), 1, "line", l, q, l < z))
        if q[1] and halved(l, z, q[0], split):
            acts.append((max(at + (4.5 if z or l < nz - 1 else 3.0 if q[0] < maps // 2 - 1 else 0.3), 17.0 + 1.5 * min(spread, 2), rising), 2, "other", l, q, l < z))
            spread += 1
    for at, l, q, up in sends:
        acts.append((at - 1.19 if at else 0.0, 3 if at else 0, "own", l, q, up))
    acts.append((KZ if z in (0, nz - 1) else KZ + 4.0, 4, "kz", 0, (0, True), True))
    acts.append((KS if z in (0, nz - 1) else KS + 2.4, 4, "ks", 0, (0, True), True))
    swaps = [v for (l, q), v in arrive.items() if q[1] and halved(l, z, q[0], split)]
    entries = [(g, part) for g in range(1, groups) for part in range(parts)]
    if z == nz - 1:
        first, then, gap = [13.5, 17.9], 25.3, 1.0
    elif z == 0:
        first, then, gap = [15.5, 18.5, 21.5, 24.5], max(swaps, default=0.0) + 0.1, 0.1
    else:
        first, then, gap = [15.5, 17.0], 19.5, 3.0
    for i, (g, part) in enumerate(entries):
        at = first[i] if i < len(first) else then + gap * (i - len(first))
        acts.append((at, 5, "in", g, (part, True), True))
    return sorted(acts, key=lambda a: a[:2])


def schedule(nz, maps, groups, parts, split):
    arrive, sends = line_arrivals(nz, maps, split)
    plans = []
    for z in range(nz):
        acts = transfers(z, arrive[z], sends[z], nz, maps, groups, parts, split)
        before = [a for a in acts if a[0] <= READY]
        rest = [a for a in acts if a[0] > READY]
        now, slots, order = READY, {}, []
        done = [0] * groups
        x_at = [0.0] + [a[0] + 5.0 for a in acts if a[2] == "in" and a[4][0] == parts - 1]
        opened = set()
        while len(order) < nz * groups:
            t = len(order)
            while rest and rest[0][0] <= now + 0.3:
                slots.setdefault(t, []).append(rest.pop(0))
            held = {a[3] for a in rest if a[2] in ("line", "other")}
            can = [g for g in range(groups) if done[g] < nz and done[g] not in held and (done[g] or x_at[g] <= now)]
            if not can:
                now = min([a[0] for a in rest[:1]] + [x for g, x in enumerate(x_at) if not done[g] and x > now])
                continue
            if z == nz - 1:
                g = min(can, key=lambda v: (v > 1 or done[v] > 1, v))
            else:
                g = min(can, key=lambda v: (done[v] < 2 and min(done) < 2 and v > 1, v))
            order.append((done[g], g, done[g] not in opened))
            opened.add(done[g])
            done[g] += 1
            now += STEP
        if rest:
            slots.setdefault(len(order) - 1, []).extend(rest)
        plans.append((before, slots, order))
    return plans


def packed(order, layers, groups):
    base = 2 * layers * groups
    per = 1
    while base ** (per + 1) < 2**30:
        per += 1
    digits = [(l * groups + g) * 2 + int(new) for l, g, new in order]
    chunks = [digits[i : i + per] for i in range(0, len(digits), per)]
    return base, per, [sum(d * base**i for i, d in enumerate(c)) for c in chunks]


def kernel(
    n, nz, group, seq_in, f_own, g_own, k_own, scale_own, bias_own, out,
    raw, x_in, x, w, kk, scales, biases, kt, gv,
    own_sem, raw_sem, in_send, in_recv, out_send, out_recv, out_own,
    w_send, z_recv, sib_recv, kz_send, kz_recv, ks_send, ks_recv, kf_send, kf_recv,
):
    s, z = lax.axis_index("seq"), lax.axis_index("segment")
    core = lax.rem(s, 2)
    sib = s + 1 - 2 * core
    channels, _, rows, radix = x.shape
    groups = channels // group
    maps = w.shape[2]
    layers = w.shape[1]
    half = n // 2
    split = n == 8 and maps % 2 == 0 and nz > 2
    parity = lax.rem(lax.div(s, 2) + lax.div(s, 4), 2) if split else 0
    beside = (s + 2 - 4 * lax.rem(lax.div(s, 2), 2), s + 4 - 8 * lax.rem(lax.div(s, 4), 2))
    parts = 2 if group % 2 == 0 else 1
    plans = schedule(nz, maps, groups, parts, split)

    def peer(d):
        return lax.rem(s + d, n)

    def remote(src, dst, send, recv, **where):
        return pltpu.make_async_remote_copy(
            src_ref=src, dst_ref=dst, send_sem=send, recv_sem=recv,
            device_id=where, device_id_type=pl.DeviceIdType.MESH,
        )

    def in_copy(g, d, part=0, parts=1):
        t = peer(d)
        size = group // parts
        here = pl.ds(g * group + part * size, size)
        return remote(x_in.at[t, here], x.at[here, s], in_send, in_recv.at[g], seq=t)

    def out_copy(c, size, d):
        t = peer(d)
        here = pl.ds(c, size)
        return remote(x.at[here, t], out.at[s, here], out_send, out_recv, seq=t)

    def z_copy(l, i, up):
        v = w.at[core, l, i]
        return remote(v, v, w_send, z_recv.at[l, i], segment=z + 1 if up else z - 1)

    def ex_copy(l, i, j):
        v = w.at[core, l, i]
        return remote(v, v, w_send, z_recv.at[l, i], seq=jnp.where(lax.rem(core + j, 2) == 0, beside[0], beside[1]))

    def sib_copy(l, r):
        v = w.at[core, l, r]
        return remote(v, v, w_send, sib_recv.at[l], seq=sib)

    def sib_wait(l):
        v = w.at[1 - core, l]
        remote(v, v, w_send, sib_recv.at[l], seq=sib).wait_recv()

    def kz_copy(d, l):
        to = lax.rem(z + d, nz)
        return tuple(
            remote(v, v, kz_send.at[i], kz_recv.at[i], segment=to)
            for i, v in enumerate((kk.at[s, l], scales.at[l], biases.at[l]))
        )

    def kz_all():
        others = pl.ds(0, nz - 1)
        return tuple(
            remote(v, v, kz_send.at[i], kz_recv.at[i], segment=lax.rem(z + 1, nz))
            for i, v in enumerate((kk.at[s, others], scales.at[others], biases.at[others]))
        )

    def ks_copy(d, owner):
        v = kk.at[owner]
        return remote(v, v, ks_send, ks_recv, seq=lax.rem(s + 2 * d, n))

    def ks_all():
        v = kk.at[pl.ds(0, half - 1)]
        return remote(v, v, ks_send, ks_recv, seq=sib)

    def kf_copy(owner):
        v = kk.at[owner]
        return remote(v, v, kf_send, kf_recv, seq=sib)

    def kf_all():
        v = kk.at[pl.ds(0, half)]
        return remote(v, v, kf_send, kf_recv, seq=sib)

    def in_wait(g):
        v = x.at[pl.ds(g * group, group), pl.ds(0, n - 1)]
        remote(v, v, in_send, in_recv.at[g], seq=sib).wait_recv()

    own = [
        pltpu.make_async_copy(f_own.at[0], w.at[0, z], own_sem.at[0]),
        pltpu.make_async_copy(g_own.at[0], w.at[1, z], own_sem.at[1]),
        pltpu.make_async_copy(k_own.at[0], kk.at[s, z], own_sem.at[2]),
        pltpu.make_async_copy(scale_own, scales.at[z], own_sem.at[3]),
        pltpu.make_async_copy(bias_own, biases.at[z], own_sem.at[4]),
    ]
    def raw_copy(d):
        t = peer(d)
        return pltpu.make_async_copy(seq_in.at[:, t], raw.at[t], raw_sem.at[d])

    for c in own:
        c.start()
    for d in range(1, n + 1):
        raw_copy(d % n).start()

    barrier = pltpu.get_barrier_semaphore()
    mesh_id = pl.DeviceIdType.MESH

    def greet(d, _):
        pl.semaphore_signal(barrier, inc=1, device_id={"seq": peer(d)}, device_id_type=mesh_id)
        return 0

    lax.fori_loop(1, n, greet, 0)

    def greet_z(d, _):
        to = lax.rem(z + d, nz)
        pl.semaphore_signal(barrier, inc=1, device_id={"segment": to}, device_id_type=mesh_id)
        return 0

    lax.fori_loop(1, nz, greet_z, 0)
    pl.semaphore_wait(barrier, n + nz - 2)

    for c in own:
        c.wait()

    def give_k(d):
        for c in kz_copy(d, z):
            c.start()

    give_k(nz - 1)

    @pl.when(z > 0)
    def _():
        for d in range(1, nz - 1):
            give_k(d)

    def send_in(g, part):
        def one(d, _):
            in_copy(g, d, part, parts).start()
            return 0

        lax.fori_loop(1, n, one, 0)

    def turned(d):
        raw_copy(d).wait()
        v = raw[peer(d)]
        return jnp.swapaxes(v, 0, 1)

    def turn(d, _):
        x_in[peer(d)] = turned(d)

        @pl.when(d > 1)
        def _():
            in_copy(0, d - 1).start()

        return 0

    def mine(q):
        return 2 * q[0] + (parity if q[1] else 1 - parity)

    def act(zz, kind, l, q, up):
        if kind == "own":
            z_copy(l, mine(q), up).start()
        elif kind == "line":
            i = mine(q)
            c = z_copy(l, i, up)
            c.wait_recv()
            if passes(l, q, zz, nz, maps, split):
                c.start()
            if q[1] and halved(l, zz, q[0], split):
                ex_copy(l, i, q[0]).start()
            sib_copy(l, i).start()
        elif kind == "other":
            i = 2 * q[0] + 1 - parity
            ex_copy(l, i, q[0]).wait_recv()
            sib_copy(l, i).start()
        elif kind == "kz":
            for c in kz_all():
                c.wait_recv()
            for d in range(1, half):
                ks_copy(d, s).start()
            kf_copy(s).start()
        elif kind == "ks":
            ks_all().wait_recv()
            for d in range(1, half):
                kf_copy(lax.rem(s + n - 2 * d, n)).start()
        elif kind == "in":
            send_in(l, q[0])

    def act_all(zz, acts):
        for a in acts:
            act(zz, *a[2:])

    for zz, (before, _, _) in enumerate(plans):
        @pl.when(z == zz)
        def _(zz=zz, before=before):
            now = [a for a in before if not a[0]]
            if zz:
                act_all(zz, now)
            else:
                act_all(zz, [a for a in now if a[4][1]])
                for d in range(nz - 2, 0, -1):
                    give_k(d)
                act_all(zz, [a for a in now if not a[4][1]])

    lax.fori_loop(1, n, turn, 0)
    x[:, pl.ds(s, 1)] = turned(0)[:, None]
    in_copy(0, n - 1).start()

    for zz, (before, _, _) in enumerate(plans):
        @pl.when(z == zz)
        def _(zz=zz, before=before):
            act_all(zz, [a for a in before if a[0]])

    def sib_arrive(l):
        @pl.when(z != l)
        def _():
            sib_wait(l)

    def load(c):
        v = x[c]
        if rows % 16:
            v = v.astype(F32)
        return v.reshape(radix, radix).astype(BF16)

    def store(c, v):
        x[c] = v.reshape(n, rows, radix).astype(BF16)

    total = scales.shape[2]
    first_channel = (z * n + s) * channels

    def prepare(l, _):
        for i in range(2):
            full = kk[:, l, i].astype(F32).reshape(radix, radix)
            kt[l, i] = full.T * (0.5, 1.0)[i]
        pick = lax.broadcasted_iota(jnp.int32, (channels, total), 1) == (
            lax.broadcasted_iota(jnp.int32, (channels, total), 0) + first_channel
        )
        for i, values in enumerate((scales[l], biases[l])):
            col = jnp.sum(jnp.where(pick, values, 0.0), axis=1, keepdims=True)
            wide = jnp.broadcast_to(0.5 * col, (channels, radix))
            gv[l, i] = wide.reshape(channels, 1, radix)
        return 0

    def compute(l, c, size):
        ids = [c + i for i in range(size)]
        f = [w[0, l, r] for r in range(maps)]
        h = [w[1, l, r] for r in range(maps)]
        y = [dot(load(c), f[0], NT).astype(BF16) for c in ids]
        y = [(dot(h[0], v, NN) * kt[l, 0]).astype(BF16) for v in y]
        y = [dot(f[1], v, NN).astype(BF16) for v in y]
        gate = [jnp.tanh(gv[l, 0, c] * load(c).astype(F32) + gv[l, 1, c]) for c in ids]
        y = [dot(v, h[1], NT) for v in y]
        y = [(v + v * t).astype(BF16) for v, t in zip(y, gate)]
        y = [dot(v, f[2], NT).astype(BF16) for v in y]
        y = [(dot(h[2], v, NN) * kt[l, 1]).astype(BF16) for v in y]
        y = [dot(f[3], v, NN).astype(BF16) for v in y]
        for c, v in zip(ids, y):
            store(c, load(c).astype(F32) + dot(v, h[3], NT))

    kf_all().wait_recv()
    lax.fori_loop(0, layers, prepare, 0)

    def step(l, g, c, size, opening):
        @pl.when(opening)
        def _():
            in_wait(g)

        compute(l, c, size)

        @pl.when(l == layers - 1)
        def _():
            def leave(d, _):
                out_copy(c, size, d).start()
                return 0

            lax.fori_loop(1, n, leave, 0)
            here = pl.ds(c, size)
            pltpu.make_async_copy(x.at[here, s], out.at[s, here], out_own).start()

    codes = [packed(order, layers, groups) for _, _, order in plans]
    base, per = codes[0][:2]
    steps = layers * groups
    last_slot = max(t for _, slots, _ in plans for t, acts in slots.items() if acts)

    def turn_step(t, code):
        digit = lax.rem(code, base)
        l, g = lax.div(digit, 2 * groups), lax.rem(lax.div(digit, 2), groups)
        @pl.when(t <= last_slot)
        def _():
            for zz, (_, slots, _) in enumerate(plans):
                @pl.when(z == zz)
                def _(zz=zz, slots=slots):
                    for tt, acts in slots.items():
                        @pl.when(t == tt)
                        def _(acts=acts):
                            act_all(zz, acts)

        @pl.when(lax.rem(digit, 2) == 1)
        def _():
            sib_arrive(l)

        step(l, g, g * group, group, l == 0)
        return lax.div(code, base)

    def run(k, _):
        code = 0
        for zz in range(nz):
            for kk_, value in enumerate(codes[zz][2]):
                code += jnp.where(jnp.logical_and(z == zz, k == kk_), value, 0)
        lax.fori_loop(k * per, jnp.minimum(k * per + per, steps), turn_step, code)
        return 0

    lax.fori_loop(0, len(codes[0][2]), run, 0)

    for c in kz_all():
        c.wait_send()
    ks_all().wait_send()
    kf_all().wait_send()
    v = x_in.at[pl.ds(0, n - 1)]
    remote(v, v, in_send, in_recv.at[0], seq=sib).wait_send()

    def sent(count):
        while count:
            some = max(k for k in (1, maps, maps * layers) if k <= count)
            v = w.at[0, 0, 0] if some == 1 else (w.at[0, 0] if some == maps else w.at[0])
            remote(v, v, w_send, z_recv.at[0, 0], seq=sib).wait_send()
            count -= some

    for zz, (before, slots, _) in enumerate(plans):
        @pl.when(z == zz)
        def _(zz=zz, acts=before + sum(slots.values(), [])):
            count = 0
            for _, _, kind, l, q, up in acts:
                count += kind in ("own", "line", "other")
                count += kind == "line" and passes(l, q, zz, nz, maps, split)
                count += kind == "line" and q[1] and halved(l, zz, q[0], split)
            sent(count)

    v = x.at[:, pl.ds(0, n - 1)]
    remote(v, v, out_send, out_recv, seq=sib).wait_send()
    pltpu.make_async_copy(x.at[:, s], out.at[s], out_own).wait()
    v = out.at[pl.ds(0, n - 1)]
    remote(v, v, out_send, out_recv, seq=sib).wait_recv()


def turn_kernel(v, out, gone, save):
    n, width = v.shape[:2]

    def put(t):
        here = pl.ds(t * width, width)
        return pltpu.make_async_copy(gone.at[t], out.at[:, here], save.at[t])

    def one(t, _):
        gone[t] = jnp.swapaxes(v[t], 0, 1)
        put(t).start()
        return 0

    lax.fori_loop(0, n, one, 0)
    for t in range(n):
        put(t).wait()


def solution(mesh):
    n, nz = mesh.shape["seq"], mesh.shape["segment"]

    def local(sequence, first, second, kernels, scale, bias):
        rows, local_channels, radix = sequence.shape
        channels = local_channels // n
        group = min(4, channels)
        groups = channels // group
        maps = first.shape[1]
        layers = nz
        total = scale.shape[1]
        x_in = sequence.reshape(rows, n, channels, radix)
        sem = pltpu.SemaphoreType.DMA
        anywhere = pl.BlockSpec(memory_space=pl.ANY)
        result = pl.pallas_call(
            functools.partial(kernel, n, nz, group),
            out_shape=pltpu.VMEM((n, channels, rows, radix), BF16),
            in_specs=[anywhere] * 6,
            out_specs=anywhere,
            scratch_shapes=[
                pltpu.VMEM((n, rows, channels, radix), BF16),
                pltpu.VMEM((n, channels, rows, radix), BF16),
                pltpu.VMEM((channels, n, rows, radix), BF16),
                pltpu.VMEM((2, layers, maps, radix, radix), BF16),
                pltpu.VMEM((n, layers, 2, rows, radix), BF16),
                pltpu.VMEM((layers, 1, total), F32),
                pltpu.VMEM((layers, 1, total), F32),
                pltpu.VMEM((layers, 2, radix, radix), F32),
                pltpu.VMEM((layers, 2, channels, 1, radix), F32),
                sem((5,)),
                sem((n,)),
                sem(()),
                sem((groups,)),
                sem(()),
                sem(()),
                sem(()),
                sem(()),
                sem((layers, maps)),
                sem((layers,)),
                sem((3,)),
                sem((3,)),
                sem(()),
                sem(()),
                sem(()),
                sem(()),
            ],
            compiler_params=pltpu.CompilerParams(
                collective_id=0, has_side_effects=True, vmem_limit_bytes=56 * 2**20
            ),
        )(x_in, first, second, kernels, scale, bias)
        return pl.pallas_call(
            turn_kernel,
            out_shape=jax.ShapeDtypeStruct((rows, local_channels, radix), BF16),
            in_specs=[pl.BlockSpec(memory_space=pltpu.VMEM)],
            out_specs=anywhere,
            scratch_shapes=[pltpu.VMEM((n, rows, channels, radix), BF16), sem((n,))],
        )(pltpu.with_memory_space_constraint(result, pltpu.VMEM))

    placed = (
        P("seq", "segment", None),
        P("segment", None, None, None),
        P("segment", None, None, None),
        P("segment", None, "seq", None),
        P("segment", None),
        P("segment", None),
    )
    return jax.shard_map(
        local, mesh=mesh, in_specs=placed, out_specs=P("seq", "segment", None), check_vma=False
    )
```

```python
import functools

import jax
import jax.numpy as jnp
from jax import lax
from jax.experimental import pallas as pl
from jax.experimental.pallas import tpu as pltpu
from jax.sharding import PartitionSpec as P

F32, BF16 = jnp.float32, jnp.bfloat16
NT = (((1,), (1,)), ((), ()))
NN = (((1,), (0,)), ((), ()))


def dot(a, b, dims):
    return lax.dot_general(a, b, dims, preferred_element_type=F32)


T0, WIRE, HOP, STEP, KZ, KS, READY = 5.0, 2.85, 1.4, 1.8, 7.5, 15.5, 18.0


def halved(l, z, j, split):
    return split and not (j > 0 and (abs(l - z) == 1 or (z == 0 and l == 2)))


def pieces(l, z, maps, split):
    pairs = range(maps // 2)
    if not split:
        return [(j, own) for j in pairs for own in (True, False)]
    return [(j, True) for j in pairs] + [(j, False) for j in pairs if not halved(l, z, j, split)]


def line_arrivals(nz, maps, split):
    arrive = [dict() for _ in range(nz)]
    sends = [[] for _ in range(nz)]
    for up in (True, False):
        path = range(nz - 1) if up else range(nz - 1, 0, -1)
        for z in path:
            to = z + 1 if up else z - 1
            own = pieces(z, to, maps, split)
            lead = len(own) if not up or z == 0 else 1
            free, queue = (T0 if z or not up else T0 - 1.6), [(T0, z, q) for q in own[:lead]]
            below = range(z) if up else range(z + 1, nz)
            relays = sorted((arrive[z][l, q], l, q) for l in below for q in pieces(l, to, maps, split))
            queue += relays
            last = relays[-1][0] if relays else T0
            queue += [(last, z, q) for q in own[lead:]]
            for at, l, q in queue:
                free = max(free, at) + WIRE
                arrive[to][l, q] = free + HOP
                if l == z:
                    sends[z].append((0.0 if at == T0 else at, l, q, up))
    return arrive, sends


def passes(l, q, z, nz, maps, split):
    to = z + 1 if l < z else z - 1
    return l != z and 0 <= to < nz and q in pieces(l, to, maps, split)


def transfers(z, arrive, sends, nz, maps, groups, parts, split):
    acts, spread = [], 0
    rising = max([at for (l, q), at in arrive.items() if l < z and passes(l, q, z, nz, maps, split)], default=0.0) - 1.15
    for (l, q), at in sorted(arrive.items(), key=lambda v: v[1]):
        acts.append((at - (1.2 if passes(l, q, z, nz, maps, split) else 0.0), 1, "line", l, q, l < z))
        if q[1] and halved(l, z, q[0], split):
            acts.append((max(at + (4.5 if z or l < nz - 1 else 3.0 if q[0] < maps // 2 - 1 else 0.3), 17.0 + 1.5 * min(spread, 2), rising), 2, "other", l, q, l < z))
            spread += 1
    for at, l, q, up in sends:
        acts.append((at - 1.19 if at else 0.0, 3 if at else 0, "own", l, q, up))
    acts.append((KZ if z in (0, nz - 1) else KZ + 4.0, 4, "kz", 0, (0, True), True))
    acts.append((KS if z in (0, nz - 1) else KS + 2.4, 4, "ks", 0, (0, True), True))
    swaps = [v for (l, q), v in arrive.items() if q[1] and halved(l, z, q[0], split)]
    entries = [(g, part) for g in range(1, groups) for part in range(parts)]
    if z == nz - 1:
        first, then, gap = [13.5, 17.9], 25.3, 1.0
    elif z == 0:
        first, then, gap = [15.5, 18.5, 21.5, 24.5], max(swaps, default=0.0), 0.0
    else:
        first, then, gap = [15.5, 17.0], 19.5, 3.0
    for i, (g, part) in enumerate(entries):
        at = first[i] if i < len(first) else then + gap * (i - len(first))
        acts.append((at, 5, "in", g, (part, True), True))
    return sorted(acts, key=lambda a: a[:2])


def schedule(nz, maps, groups, parts, split):
    arrive, sends = line_arrivals(nz, maps, split)
    plans = []
    for z in range(nz):
        acts = transfers(z, arrive[z], sends[z], nz, maps, groups, parts, split)
        before = [a for a in acts if a[0] <= READY]
        rest = [a for a in acts if a[0] > READY]
        now, slots, order = READY, {}, []
        done = [0] * groups
        x_at = [0.0] + [a[0] + 5.0 for a in acts if a[2] == "in" and a[4][0] == parts - 1]
        opened = set()
        while len(order) < nz * groups:
            t = len(order)
            while rest and rest[0][0] <= now + 0.3:
                slots.setdefault(t, []).append(rest.pop(0))
            held = {a[3] for a in rest if a[2] in ("line", "other")}
            can = [g for g in range(groups) if done[g] < nz and done[g] not in held and (done[g] or x_at[g] <= now)]
            if not can:
                now = min([a[0] for a in rest[:1]] + [x for g, x in enumerate(x_at) if not done[g] and x > now])
                continue
            if z == nz - 1:
                g = min(can, key=lambda v: (v > 1 or done[v] > 1, v))
            else:
                g = min(can, key=lambda v: (done[v] < 2 and min(done) < 2 and v > 1, v))
            order.append((done[g], g, done[g] not in opened))
            opened.add(done[g])
            done[g] += 1
            now += STEP
        if rest:
            slots.setdefault(len(order) - 1, []).extend(rest)
        plans.append((before, slots, order))
    return plans


def packed(order, layers, groups):
    base = 2 * layers * groups
    per = 1
    while base ** (per + 1) < 2**30:
        per += 1
    digits = [(l * groups + g) * 2 + int(new) for l, g, new in order]
    chunks = [digits[i : i + per] for i in range(0, len(digits), per)]
    return base, per, [sum(d * base**i for i, d in enumerate(c)) for c in chunks]


def kernel(
    n, nz, group, seq_in, f_own, g_own, k_own, scale_own, bias_own, out,
    raw, x_in, x, w, kk, scales, biases, kt, gv,
    own_sem, raw_sem, in_send, in_recv, out_send, out_recv, out_own,
    w_send, z_recv, sib_recv, kz_send, kz_recv, ks_send, ks_recv, kf_send, kf_recv,
):
    s, z = lax.axis_index("seq"), lax.axis_index("segment")
    core = lax.rem(s, 2)
    sib = s + 1 - 2 * core
    channels, _, rows, radix = x.shape
    groups = channels // group
    maps = w.shape[2]
    layers = w.shape[1]
    half = n // 2
    split = n == 8 and maps % 2 == 0 and nz > 2
    parity = lax.rem(lax.div(s, 2) + lax.div(s, 4), 2) if split else 0
    beside = (s + 2 - 4 * lax.rem(lax.div(s, 2), 2), s + 4 - 8 * lax.rem(lax.div(s, 4), 2))
    parts = 2 if group % 2 == 0 else 1
    plans = schedule(nz, maps, groups, parts, split)

    def peer(d):
        return lax.rem(s + d, n)

    def remote(src, dst, send, recv, **where):
        return pltpu.make_async_remote_copy(
            src_ref=src, dst_ref=dst, send_sem=send, recv_sem=recv,
            device_id=where, device_id_type=pl.DeviceIdType.MESH,
        )

    def in_copy(g, d, part=0, parts=1):
        t = peer(d)
        size = group // parts
        here = pl.ds(g * group + part * size, size)
        return remote(x_in.at[t, here], x.at[here, s], in_send, in_recv.at[g], seq=t)

    def out_copy(c, size, d):
        t = peer(d)
        here = pl.ds(c, size)
        return remote(x.at[here, t], out.at[s, here], out_send, out_recv, seq=t)

    def z_copy(l, i, up):
        v = w.at[core, l, i]
        return remote(v, v, w_send, z_recv.at[l, i], segment=z + 1 if up else z - 1)

    def ex_copy(l, i, j):
        v = w.at[core, l, i]
        return remote(v, v, w_send, z_recv.at[l, i], seq=jnp.where(lax.rem(core + j, 2) == 0, beside[0], beside[1]))

    def sib_copy(l, r):
        v = w.at[core, l, r]
        return remote(v, v, w_send, sib_recv.at[l], seq=sib)

    def sib_wait(l):
        v = w.at[1 - core, l]
        remote(v, v, w_send, sib_recv.at[l], seq=sib).wait_recv()

    def kz_copy(d, l):
        to = lax.rem(z + d, nz)
        return tuple(
            remote(v, v, kz_send.at[i], kz_recv.at[i], segment=to)
            for i, v in enumerate((kk.at[s, l], scales.at[l], biases.at[l]))
        )

    def kz_all():
        others = pl.ds(0, nz - 1)
        return tuple(
            remote(v, v, kz_send.at[i], kz_recv.at[i], segment=lax.rem(z + 1, nz))
            for i, v in enumerate((kk.at[s, others], scales.at[others], biases.at[others]))
        )

    def ks_copy(d, owner):
        v = kk.at[owner]
        return remote(v, v, ks_send, ks_recv, seq=lax.rem(s + 2 * d, n))

    def ks_all():
        v = kk.at[pl.ds(0, half - 1)]
        return remote(v, v, ks_send, ks_recv, seq=sib)

    def kf_copy(owner):
        v = kk.at[owner]
        return remote(v, v, kf_send, kf_recv, seq=sib)

    def kf_all():
        v = kk.at[pl.ds(0, half)]
        return remote(v, v, kf_send, kf_recv, seq=sib)

    def in_wait(g):
        v = x.at[pl.ds(g * group, group), pl.ds(0, n - 1)]
        remote(v, v, in_send, in_recv.at[g], seq=sib).wait_recv()

    own = [
        pltpu.make_async_copy(f_own.at[0], w.at[0, z], own_sem.at[0]),
        pltpu.make_async_copy(g_own.at[0], w.at[1, z], own_sem.at[1]),
        pltpu.make_async_copy(k_own.at[0], kk.at[s, z], own_sem.at[2]),
        pltpu.make_async_copy(scale_own, scales.at[z], own_sem.at[3]),
        pltpu.make_async_copy(bias_own, biases.at[z], own_sem.at[4]),
    ]
    def raw_copy(d):
        t = peer(d)
        return pltpu.make_async_copy(seq_in.at[:, t], raw.at[t], raw_sem.at[d])

    for c in own:
        c.start()
    for d in range(1, n + 1):
        raw_copy(d % n).start()

    barrier = pltpu.get_barrier_semaphore()
    mesh_id = pl.DeviceIdType.MESH

    def greet(d, _):
        pl.semaphore_signal(barrier, inc=1, device_id={"seq": peer(d)}, device_id_type=mesh_id)
        return 0

    lax.fori_loop(1, n, greet, 0)

    def greet_z(d, _):
        to = lax.rem(z + d, nz)
        pl.semaphore_signal(barrier, inc=1, device_id={"segment": to}, device_id_type=mesh_id)
        return 0

    lax.fori_loop(1, nz, greet_z, 0)
    pl.semaphore_wait(barrier, n + nz - 2)

    for c in own:
        c.wait()

    def give_k(d):
        for c in kz_copy(d, z):
            c.start()

    give_k(nz - 1)

    @pl.when(z > 0)
    def _():
        for d in range(1, nz - 1):
            give_k(d)

    def send_in(g, part):
        def one(d, _):
            in_copy(g, d, part, parts).start()
            return 0

        lax.fori_loop(1, n, one, 0)

    def turned(d):
        raw_copy(d).wait()
        v = raw[peer(d)]
        return jnp.swapaxes(v, 0, 1)

    def turn(d, _):
        x_in[peer(d)] = turned(d)

        @pl.when(d > 1)
        def _():
            in_copy(0, d - 1).start()

        return 0

    def mine(q):
        return 2 * q[0] + (parity if q[1] else 1 - parity)

    def act(zz, kind, l, q, up):
        if kind == "own":
            z_copy(l, mine(q), up).start()
        elif kind == "line":
            i = mine(q)
            c = z_copy(l, i, up)
            c.wait_recv()
            if passes(l, q, zz, nz, maps, split):
                c.start()
            if q[1] and halved(l, zz, q[0], split):
                ex_copy(l, i, q[0]).start()
            sib_copy(l, i).start()
        elif kind == "other":
            i = 2 * q[0] + 1 - parity
            ex_copy(l, i, q[0]).wait_recv()
            sib_copy(l, i).start()
        elif kind == "kz":
            for c in kz_all():
                c.wait_recv()
            for d in range(1, half):
                ks_copy(d, s).start()
            kf_copy(s).start()
        elif kind == "ks":
            ks_all().wait_recv()
            for d in range(1, half):
                kf_copy(lax.rem(s + n - 2 * d, n)).start()
        elif kind == "in":
            send_in(l, q[0])

    def act_all(zz, acts):
        for a in acts:
            act(zz, *a[2:])

    for zz, (before, _, _) in enumerate(plans):
        @pl.when(z == zz)
        def _(zz=zz, before=before):
            now = [a for a in before if not a[0]]
            if zz:
                act_all(zz, now)
            else:
                act_all(zz, [a for a in now if a[4][1]])
                for d in range(nz - 2, 0, -1):
                    give_k(d)
                act_all(zz, [a for a in now if not a[4][1]])

    lax.fori_loop(1, n, turn, 0)
    x[:, pl.ds(s, 1)] = turned(0)[:, None]
    in_copy(0, n - 1).start()

    for zz, (before, _, _) in enumerate(plans):
        @pl.when(z == zz)
        def _(zz=zz, before=before):
            act_all(zz, [a for a in before if a[0]])

    def sib_arrive(l):
        @pl.when(z != l)
        def _():
            sib_wait(l)

    def load(c):
        v = x[c]
        if rows % 16:
            v = v.astype(F32)
        return v.reshape(radix, radix).astype(BF16)

    def store(c, v):
        x[c] = v.reshape(n, rows, radix).astype(BF16)

    total = scales.shape[2]
    first_channel = (z * n + s) * channels

    def prepare(l, _):
        for i in range(2):
            full = kk[:, l, i].astype(F32).reshape(radix, radix)
            kt[l, i] = full.T * (0.5, 1.0)[i]
        pick = lax.broadcasted_iota(jnp.int32, (channels, total), 1) == (
            lax.broadcasted_iota(jnp.int32, (channels, total), 0) + first_channel
        )
        for i, values in enumerate((scales[l], biases[l])):
            col = jnp.sum(jnp.where(pick, values, 0.0), axis=1, keepdims=True)
            wide = jnp.broadcast_to(0.5 * col, (channels, radix))
            gv[l, i] = wide.reshape(channels, 1, radix)
        return 0

    def compute(l, c, size):
        ids = [c + i for i in range(size)]
        f = [w[0, l, r] for r in range(maps)]
        h = [w[1, l, r] for r in range(maps)]
        y = [dot(load(c), f[0], NT).astype(BF16) for c in ids]
        y = [(dot(h[0], v, NN) * kt[l, 0]).astype(BF16) for v in y]
        y = [dot(f[1], v, NN).astype(BF16) for v in y]
        gate = [jnp.tanh(gv[l, 0, c] * load(c).astype(F32) + gv[l, 1, c]) for c in ids]
        y = [dot(v, h[1], NT) for v in y]
        y = [(v + v * t).astype(BF16) for v, t in zip(y, gate)]
        y = [dot(v, f[2], NT).astype(BF16) for v in y]
        y = [(dot(h[2], v, NN) * kt[l, 1]).astype(BF16) for v in y]
        y = [dot(f[3], v, NN).astype(BF16) for v in y]
        for c, v in zip(ids, y):
            store(c, load(c).astype(F32) + dot(v, h[3], NT))

    kf_all().wait_recv()
    lax.fori_loop(0, layers, prepare, 0)

    def step(l, g, c, size, opening):
        @pl.when(opening)
        def _():
            in_wait(g)

        compute(l, c, size)

        @pl.when(l == layers - 1)
        def _():
            def leave(d, _):
                out_copy(c, size, d).start()
                return 0

            lax.fori_loop(1, n, leave, 0)
            here = pl.ds(c, size)
            pltpu.make_async_copy(x.at[here, s], out.at[s, here], out_own).start()

    codes = [packed(order, layers, groups) for _, _, order in plans]
    base, per = codes[0][:2]
    steps = layers * groups
    last_slot = max(t for _, slots, _ in plans for t, acts in slots.items() if acts)

    def turn_step(t, code):
        digit = lax.rem(code, base)
        l, g = lax.div(digit, 2 * groups), lax.rem(lax.div(digit, 2), groups)
        @pl.when(t <= last_slot)
        def _():
            for zz, (_, slots, _) in enumerate(plans):
                @pl.when(z == zz)
                def _(zz=zz, slots=slots):
                    for tt, acts in slots.items():
                        @pl.when(t == tt)
                        def _(acts=acts):
                            act_all(zz, acts)

        @pl.when(lax.rem(digit, 2) == 1)
        def _():
            sib_arrive(l)

        step(l, g, g * group, group, l == 0)
        return lax.div(code, base)

    def run(k, _):
        code = 0
        for zz in range(nz):
            for kk_, value in enumerate(codes[zz][2]):
                code += jnp.where(jnp.logical_and(z == zz, k == kk_), value, 0)
        lax.fori_loop(k * per, jnp.minimum(k * per + per, steps), turn_step, code)
        return 0

    lax.fori_loop(0, len(codes[0][2]), run, 0)

    for c in kz_all():
        c.wait_send()
    ks_all().wait_send()
    kf_all().wait_send()
    v = x_in.at[pl.ds(0, n - 1)]
    remote(v, v, in_send, in_recv.at[0], seq=sib).wait_send()

    def sent(count):
        while count:
            some = max(k for k in (1, maps, maps * layers) if k <= count)
            v = w.at[0, 0, 0] if some == 1 else (w.at[0, 0] if some == maps else w.at[0])
            remote(v, v, w_send, z_recv.at[0, 0], seq=sib).wait_send()
            count -= some

    for zz, (before, slots, _) in enumerate(plans):
        @pl.when(z == zz)
        def _(zz=zz, acts=before + sum(slots.values(), [])):
            count = 0
            for _, _, kind, l, q, up in acts:
                count += kind in ("own", "line", "other")
                count += kind == "line" and passes(l, q, zz, nz, maps, split)
                count += kind == "line" and q[1] and halved(l, zz, q[0], split)
            sent(count)

    v = x.at[:, pl.ds(0, n - 1)]
    remote(v, v, out_send, out_recv, seq=sib).wait_send()
    pltpu.make_async_copy(x.at[:, s], out.at[s], out_own).wait()
    v = out.at[pl.ds(0, n - 1)]
    remote(v, v, out_send, out_recv, seq=sib).wait_recv()


def turn_kernel(v, out, gone, save):
    n, width = v.shape[:2]

    def put(t):
        here = pl.ds(t * width, width)
        return pltpu.make_async_copy(gone.at[t], out.at[:, here], save.at[t])

    def one(t, _):
        gone[t] = jnp.swapaxes(v[t], 0, 1)
        put(t).start()
        return 0

    lax.fori_loop(0, n, one, 0)
    for t in range(n):
        put(t).wait()


def solution(mesh):
    n, nz = mesh.shape["seq"], mesh.shape["segment"]

    def local(sequence, first, second, kernels, scale, bias):
        rows, local_channels, radix = sequence.shape
        channels = local_channels // n
        group = min(4, channels)
        groups = channels // group
        maps = first.shape[1]
        layers = nz
        total = scale.shape[1]
        x_in = sequence.reshape(rows, n, channels, radix)
        sem = pltpu.SemaphoreType.DMA
        anywhere = pl.BlockSpec(memory_space=pl.ANY)
        result = pl.pallas_call(
            functools.partial(kernel, n, nz, group),
            out_shape=pltpu.VMEM((n, channels, rows, radix), BF16),
            in_specs=[anywhere] * 6,
            out_specs=anywhere,
            scratch_shapes=[
                pltpu.VMEM((n, rows, channels, radix), BF16),
                pltpu.VMEM((n, channels, rows, radix), BF16),
                pltpu.VMEM((channels, n, rows, radix), BF16),
                pltpu.VMEM((2, layers, maps, radix, radix), BF16),
                pltpu.VMEM((n, layers, 2, rows, radix), BF16),
                pltpu.VMEM((layers, 1, total), F32),
                pltpu.VMEM((layers, 1, total), F32),
                pltpu.VMEM((layers, 2, radix, radix), F32),
                pltpu.VMEM((layers, 2, channels, 1, radix), F32),
                sem((5,)),
                sem((n,)),
                sem(()),
                sem((groups,)),
                sem(()),
                sem(()),
                sem(()),
                sem(()),
                sem((layers, maps)),
                sem((layers,)),
                sem((3,)),
                sem((3,)),
                sem(()),
                sem(()),
                sem(()),
                sem(()),
            ],
            compiler_params=pltpu.CompilerParams(
                collective_id=0, has_side_effects=True, vmem_limit_bytes=56 * 2**20
            ),
        )(x_in, first, second, kernels, scale, bias)
        return pl.pallas_call(
            turn_kernel,
            out_shape=jax.ShapeDtypeStruct((rows, local_channels, radix), BF16),
            in_specs=[pl.BlockSpec(memory_space=pltpu.VMEM)],
            out_specs=anywhere,
            scratch_shapes=[pltpu.VMEM((n, rows, channels, radix), BF16), sem((n,))],
        )(pltpu.with_memory_space_constraint(result, pltpu.VMEM))

    placed = (
        P("seq", "segment", None),
        P("segment", None, None, None),
        P("segment", None, None, None),
        P("segment", None, "seq", None),
        P("segment", None),
        P("segment", None),
    )
    return jax.shard_map(
        local, mesh=mesh, in_specs=placed, out_specs=P("seq", "segment", None), check_vma=False
    )
```
